256 devices in a mesh: rows: 32 (over z, x), cols: 8 (over y, core).
Axes of the slice: x: 4, y: 4, z: 8, core: 2. Of those that a mesh axis runs over, the one named last changes fastest.
Arguments:
- features: bfloat16 [524288, 440], P(('rows', 'cols')), may hold values from -12 to 12
- residual: float32 [524288, 147], P(('rows', 'cols')), may hold values from -6 to 6
- coeffs: float32 [524288, 147], P(('rows', 'cols')), may hold values from -3 to 3
- block_inverse: float32 [2, 2048, 2048], P(None, ('rows', 'cols')), may hold values from -0.0234375 to 0.0234375
- block_index: int32 [2, 2048], P(None, 'cols'), may hold values from 0 to 2047, as said below
- owners: int32 [2], replicated, may hold values from 0 to 31
Outputs:
- new_coeffs: float32 [524288, 147], P(('rows', 'cols'))
- new_residual: float32 [524288, 147], P(('rows', 'cols'))
The draws below stay inside these ranges and needn't reach their ends.
Inputs may be any that keep to these rules, and one draw needn't show every extreme that they name: `block_index`: for each step and each aligned run of 256 positions, the indices are distinct.
All inputs are finite; a program needn't handle non-finite values.
Results may differ from the reference program's by a relative error of at most 0.0028.
Values may be sent and summed in bfloat16 or wider, within the bound.
A program may use at most 64 MiB of HBM per device.

```python
import jax
import jax.numpy as jnp
from jax import lax

D = 440
C = 147
BLOCK = 2048
STEPS = 2
FRAMES_DEV = 2048
FRAMES = 524288
PICK = 256
N_ROWS = 32
N_COLS = 8


def draw_block_index(key, part):
    per_col = BLOCK // N_COLS
    streams = jax.random.split(jax.random.fold_in(key, 17), STEPS * N_COLS)
    picked = jax.vmap(lambda stream: jax.random.permutation(stream, FRAMES_DEV)[:per_col])(streams)
    return picked.reshape(STEPS, BLOCK).astype(jnp.int32)


def draw_features(key, part):
    latent_width = 32
    cluster_count = 64
    streams = [jax.random.fold_in(key, 211 + offset) for offset in range(8)]
    mixing = jax.random.normal(streams[0], (latent_width, D), jnp.float32) / jnp.sqrt(float(latent_width))
    centres = jax.random.normal(streams[1], (cluster_count, latent_width), jnp.float32)
    member = jax.random.randint(streams[2], (FRAMES,), 0, cluster_count)
    spread = jnp.full((cluster_count, 1), 0.3, jnp.float32)
    local_part = jax.random.normal(streams[5], (FRAMES, latent_width), jnp.float32)
    jitter_scale = jnp.exp(jax.random.uniform(streams[7], (FRAMES, 1), jnp.float32, jnp.log(0.4), jnp.log(1.0)))
    frame_latent = centres[member] + local_part * spread[member]
    jitter = jitter_scale * jax.random.normal(streams[6], (FRAMES, D), jnp.float32)
    mixed = jnp.dot(frame_latent, mixing, precision=jax.lax.Precision.HIGHEST) + jitter
    return jnp.clip(mixed, -12.0, 12.0).astype(jnp.bfloat16)


def shard_levels(key, dims, cuts, smallest, top_value):
    def one(position, blocks):
        draws = jax.random.uniform(jax.random.fold_in(jax.random.fold_in(key, 6), position), (blocks,), jnp.float32, smallest / len(cuts), top_value / len(cuts))
        return jnp.repeat(jnp.exp(draws), dims[position] // blocks).reshape((-1,) + (1,) * (len(dims) - position - 1))

    factor_of = one(*cuts[0])
    for cut in cuts[1:]:
        factor_of = factor_of * one(*cut)
    return factor_of


def noise(key, dims, deviation, bound, cuts=(), held_as=jnp.bfloat16):
    values = deviation * jax.random.normal(key, dims, jnp.float32)
    if cuts:
        values = values * shard_levels(key, dims, cuts, -0.22, 0.18)
    return jnp.clip(values, -bound, bound).astype(held_as)


def setup_inputs(seed: int = 0) -> dict:
    arg_keys = jax.random.split(jax.random.key(seed), 7)
    return {
        "features": draw_features(jax.random.fold_in(arg_keys[6], 71), 0),
        "residual": noise(arg_keys[1], (FRAMES, C), 1.0, 6.0, ((0, 256),), jnp.float32),
        "coeffs": noise(arg_keys[2], (FRAMES, C), 0.5, 3.0, ((0, 256),), jnp.float32),
        "block_inverse": noise(arg_keys[3], (STEPS, BLOCK, BLOCK), (36 * BLOCK) ** -0.5, 0.0234375, ((1, 256),), jnp.float32),
        "block_index": draw_block_index(jax.random.fold_in(arg_keys[6], 71), 0),
        "owners": jax.random.randint(arg_keys[5], (STEPS,), 0, N_ROWS).astype(jnp.int32),
    }


def reference(features, residual, coeffs, block_inverse, block_index, owners):
    total = features.shape[0]
    squares = jnp.sum(jnp.square(features.astype(jnp.float32)), axis=1)
    row_block = min(4096, total)
    feature_blocks = features.reshape(total // row_block, row_block, D)
    norm_blocks = squares.reshape(total // row_block, row_block)
    column_group = (jnp.arange(BLOCK) // PICK).astype(jnp.int32)
    for step_id in range(STEPS):
        points = ((owners[step_id] * N_COLS + column_group) * FRAMES_DEV + block_index[step_id]).astype(jnp.int32)
        chosen = features[points]
        chosen_norms = squares[points]
        update = jnp.dot(block_inverse[step_id], residual[points], precision=lax.Precision.HIGHEST,
                         preferred_element_type=jnp.float32).astype(jnp.bfloat16)

        def kernel_rows(operands):
            block_rows, block_norms = operands
            inner = jnp.dot(block_rows, chosen.T, preferred_element_type=jnp.float32)
            distance = block_norms[:, None] + chosen_norms[None, :] - 2.0 * inner
            kernel = jnp.exp(distance * (-1.0 / D)).astype(jnp.bfloat16)
            return jnp.dot(kernel, update, preferred_element_type=jnp.float32)

        change = lax.map(kernel_rows, (feature_blocks, norm_blocks)).reshape(total, C)
        residual = residual - change
        residual = residual.at[points].add(-0.5 * update.astype(jnp.float32))
        coeffs = coeffs.at[points].add(update.astype(jnp.float32))
    return coeffs, residual
```

```python
import functools
import math

import jax
import jax.numpy as jnp
from jax import lax
from jax.experimental import pallas as pl
from jax.experimental.pallas import tpu as pltpu
from jax.sharding import PartitionSpec as P

MESH = pl.DeviceIdType.MESH
NZ, NX, NY, NK = 8, 4, 4, 2
PICK = 256
BLOCK = 2048
PAD_D = 512
PAD_C = 256
TILE = 256
F32 = jnp.float32
BF16 = jnp.bfloat16

STAGES = {
    "r_rsx": 4, "r_rsz": 8, "r_agz": 8, "r_agx": 4,
    "y_rsx": 8, "y_rsz": 8, "y_agz": 8, "y_ag2": 4, "y_ag3": 16, "y_core": 16,
    "p": 8, "u_agz": 8, "u_ag2": 4, "u_ag3": 16, "u_core": 16,
}
BASE = {}
_total = 0
for _name, _count in STAGES.items():
    BASE[_name] = _total
    _total += 2 * _count
BASE["b"] = _total
N_SEMS = _total + 8


def split3(value):
    hi = value.astype(BF16)
    rest = value - hi.astype(F32)
    mid = rest.astype(BF16)
    lo = (rest - mid.astype(F32)).astype(BF16)
    return hi.astype(F32), mid.astype(F32), lo.astype(F32)


def dot_t(a, b):
    return lax.dot_general(a, b, (((1,), (1,)), ((), ())), preferred_element_type=F32)


def with_norms(tail, squares, parts_at, ones_at, axis=1):
    lane = lax.broadcasted_iota(jnp.int32, tail.shape, axis)
    hi, mid, lo = split3(-0.5 * squares)
    out = jnp.where(lane < 56, tail, 0.0)
    out = jnp.where((lane >= ones_at) & (lane < ones_at + 3), 1.0, out)
    out = jnp.where(lane == parts_at, hi, out)
    out = jnp.where(lane == parts_at + 1, mid, out)
    return jnp.where(lane == parts_at + 2, lo, out)


def body(width, outs, owners, feat, res, binv, idxr, chg, dco,
         idxc, xa, cho, rcho, rrx0, rrx1, rsel, rrz0, rrz1, rch, rbuf, rx0, rx1, sel, rz0, rz1, ych,
         ybuf, bg, pbuf, up, uch, ubuf, ut, kb, k21, ssem, rsem, lsem):
    rrx, rrz, rx, rz = (rrx0, rrx1), (rrz0, rrz1), (rx0, rx1), (rz0, rz1)
    r = lax.axis_index("rows")
    c = lax.axis_index("cols")
    z, x = r // NX, r % NX
    y, k = c // NK, c % NK
    scale = 2.0 / width * math.log2(math.e)
    khalf = pl.ds(pl.multiple_of(k * 256, 256), 256)
    klane = pl.ds(pl.multiple_of(k * 128, 128), 128)
    tail_start = 384
    tail_used = width - tail_start

    def dev(zz, xx, yy, kk):
        return (zz * NX + xx, yy * NK + kk)

    desc = {}

    def send(name, s, i, src, dst, target):
        at = BASE[name] + (s * STAGES[name] + i if name in STAGES else i)
        copy = pltpu.make_async_remote_copy(
            src_ref=src, dst_ref=dst, send_sem=ssem.at[at], recv_sem=rsem.at[at],
            device_id=target, device_id_type=MESH)
        copy.start()
        desc[(name, s, i)] = copy

    def arrived(name, s, i):
        desc[(name, s, i)].wait_recv()

    local_count = [0]

    def local(src, dst):
        copy = pltpu.make_async_copy(src, dst, lsem.at[local_count[0]])
        local_count[0] += 1
        copy.start()
        return copy

    peers = []
    for i in range(NX):
        for kk in range(NK):
            if (i, kk) != (0, 0):
                peers.append(dev(z, (x + i) % NX, y, (k + kk) % NK))
    for i in range(1, NZ):
        peers.append(dev((z + i) % NZ, x, y, k))
    for i in range(1, NY):
        for kk in range(NK):
            peers.append(dev(z, x, (y + i) % NY, (k + kk) % NK))
    barrier = pltpu.get_barrier_semaphore()
    for peer in peers:
        pl.semaphore_signal(barrier, inc=1, device_id=peer, device_id_type=MESH)

    rcho[...] = jnp.zeros_like(rcho)
    res_hi = res[...].astype(BF16)
    res_lo = (res[...] - res_hi.astype(F32)).astype(BF16)
    diagonal = (lax.broadcasted_iota(jnp.int32, (PICK, PICK), 0)
                == lax.broadcasted_iota(jnp.int32, (PICK, PICK), 1))

    def chosen_at(s):
        index = jnp.broadcast_to(idxr[s:s + 1, :], (PICK, PICK))
        return jnp.sum(jnp.where(diagonal, index, 0).astype(F32), axis=1,
                       keepdims=True).astype(jnp.int32)

    def picks(s, start, size):
        position = lax.broadcasted_iota(jnp.int32, (PICK, size), 1) + start
        return jnp.where(idxc[s] == position, 1.0, 0.0)

    for s in range(2):
        idxc[s] = chosen_at(s)
        pick = picks(s, 0, BLOCK).astype(BF16)
        rcho[s, :, 0:outs] = dot_t(pick, res_hi) + dot_t(pick, res_lo)
        rows = dot_t(pick, feat[...])
        squares = jnp.sum(rows * rows, axis=1, keepdims=True)
        cho[s, :, 0:width] = rows.astype(BF16)
        cho[s, :, tail_start:PAD_D] = with_norms(
            cho[s, :, tail_start:PAD_D].astype(F32), squares, tail_used + 3, tail_used).astype(BF16)

    pl.semaphore_wait(barrier, len(peers))

    waits = {}

    def r_rsx(s):
        for i in range(1, NX):
            xx = (x + i) % NX
            send("r_rsx", s, i, rcho.at[s, pl.ds(pl.multiple_of(xx * 64, 64), 64), :],
                 rrx[s].at[x], dev(z, xx, y, k))
        waits[("r_rsx", s)] = local(
            rcho.at[s, pl.ds(pl.multiple_of(x * 64, 64), 64), :], rrx[s].at[x])

    def y_rsx(s):
        for i in range(NX):
            xx = (x + i) % NX
            for kk in range(NK):
                if (i, kk) == (0, 0):
                    continue
                k2 = (k + kk) % NK
                send("y_rsx", s, i * NK + kk,
                     cho.at[s, pl.ds(pl.multiple_of(xx * 64, 64), 64),
                            pl.ds(pl.multiple_of(k2 * 256, 256), 256)],
                     rx[s].at[x, k], dev(z, xx, y, k2))
        waits[("y_rsx", s)] = local(
            cho.at[s, pl.ds(pl.multiple_of(x * 64, 64), 64), khalf], rx[s].at[x, k])

    def r_rsz(s):
        for i in range(1, NX):
            arrived("r_rsx", s, i)
        waits[("r_rsx", s)].wait()
        rsel[s] = rrx[s][owners[s] % NX]
        for i in range(NZ):
            zz = (z + i) % NZ
            src = rsel.at[s, pl.ds(pl.multiple_of(zz * 8, 8), 8), :]
            if i == 0:
                waits[("r_rsz", s)] = local(src, rrz[s].at[z])
            else:
                send("r_rsz", s, i, src, rrz[s].at[z], dev(zz, x, y, k))

    def y_rsz(s):
        for i in range(NX):
            for kk in range(NK):
                if (i, kk) != (0, 0):
                    arrived("y_rsx", s, i * NK + kk)
        waits[("y_rsx", s)].wait()
        sel[s] = rx[s][owners[s] % NX]
        for i in range(NZ):
            zz = (z + i) % NZ
            src = sel.at[s, zz // 4, pl.ds(pl.multiple_of((zz % 4) * 16, 16), 16), :]
            if i == 0:
                waits[("y_rsz", s)] = local(src, rz[s].at[z])
            else:
                send("y_rsz", s, i, src, rz[s].at[z], dev(zz, x, y, k))

    def r_agz(s):
        for i in range(1, NZ):
            arrived("r_rsz", s, i)
        waits[("r_rsz", s)].wait()
        rch[s] = rrz[s][owners[s] // NX]
        place = rbuf.at[s, pl.ds(pl.multiple_of(x * 64 + z * 8, 8), 8), :]
        for i in range(1, NZ):
            send("r_agz", s, i, rch.at[s], place, dev((z + i) % NZ, x, y, k))
        waits[("r_agz", s)] = local(rch.at[s], place)

    def y_agz(s):
        for i in range(1, NZ):
            arrived("y_rsz", s, i)
        waits[("y_rsz", s)].wait()
        ych[s] = rz[s][owners[s] // NX]
        place = ybuf.at[s, 2 * y + z // 4, x,
                        pl.ds(pl.multiple_of((z % 4) * 16, 16), 16), khalf]
        for i in range(1, NZ):
            send("y_agz", s, i, ych.at[s], place, dev((z + i) % NZ, x, y, k))
        waits[("y_agz", s)] = local(ych.at[s], place)

    def r_agx(s):
        for i in range(1, NZ):
            arrived("r_agz", s, i)
        waits[("r_agz", s)].wait()
        part = rbuf.at[s, pl.ds(pl.multiple_of(x * 64, 64), 64), :]
        for i in range(1, NX):
            send("r_agx", s, i, part, part, dev(z, (x + i) % NX, y, k))

    g = (1 - k) * x + k * y
    q = (1 - k) * y + k * x

    def y_block(s, gg, qq):
        bx = (1 - k) * gg + k * qq
        by = k * gg + (1 - k) * qq
        return ybuf.at[s, pl.ds(2 * by, 2), bx, :, khalf]

    def u_block(s, gg, qq):
        bx = (1 - k) * gg + k * qq
        by = k * gg + (1 - k) * qq
        return ubuf.at[s, :, bx, by, :, klane]

    def to_second(i):
        return dev(z, (x + i * (1 - k)) % NX, (y + i * k) % NY, k)

    def to_third(i):
        return dev(z, (x + i * k) % NX, (y + i * (1 - k)) % NY, k)

    def ring_send(kind, block, s, d):
        part = block(s, (g - d + NX) % NX, q)
        for i in range(1, NY):
            send(kind + "_ag3", s, d * 4 + i, part, part, to_third(i))
        send(kind + "_core", s, d * 4, part, part, dev(z, x, y, 1 - k))

    def ag2_start(kind, block, s):
        for i in range(1, NZ):
            arrived(kind + "_agz", s, i)
        waits[(kind + "_agz", s)].wait()
        part = block(s, g, q)
        for i in range(1, NX):
            send(kind + "_ag2", s, i, part, part, to_second(i))
        ring_send(kind, block, s, 0)

    def ag3_start(kind, block, s):
        for d in range(1, NX):
            arrived(kind + "_ag2", s, d)
            ring_send(kind, block, s, d)

    def core_start(kind, block, s):
        for d in range(NX):
            for i in range(1, NY):
                arrived(kind + "_ag3", s, d * 4 + i)
                part = block(s, (g - d + NX) % NX, (q - i + NY) % NY)
                send(kind + "_core", s, d * 4 + i, part, part, dev(z, x, y, 1 - k))

    def core_end(kind, s):
        for d in range(NX):
            for i in range(NY):
                arrived(kind + "_core", s, d * 4 + i)

    def partial_start(s, values):
        pbuf[s] = jnp.dot(bg[s], values, precision=lax.Precision.HIGHEST,
                          preferred_element_type=F32)
        for i in range(NY * NK):
            cc = (c + i) % (NY * NK)
            src = pbuf.at[s, pl.ds(pl.multiple_of((cc // NK) * 16, 16), 16),
                          pl.ds(pl.multiple_of((cc % NK) * 128, 128), 128)]
            if i == 0:
                waits[("p", s)] = local(src, up.at[s, c])
            else:
                send("p", s, i, src, up.at[s, c], (r, cc))

    def u_agz(s):
        for i in range(1, NY * NK):
            arrived("p", s, i)
        waits[("p", s)].wait()
        uch[s] = jnp.sum(up[s], axis=0).astype(BF16)
        place = ubuf.at[s, z, x, y, :, klane]
        for i in range(1, NZ):
            send("u_agz", s, i, uch.at[s], place, dev((z + i) % NZ, x, y, k))
        waits[("u_agz", s)] = local(uch.at[s], place)

    def gen(s, first, last):
        @pl.loop(first, last)
        def _(t):
            at = pl.ds(pl.multiple_of(t * TILE, TILE), TILE)
            points = ybuf[s, t].reshape(TILE, PAD_D)
            for j in range(4):
                inner = jnp.dot(points, xa[:, j * 512:(j + 1) * 512], preferred_element_type=F32)
                kb[s, at, j * 512:(j + 1) * 512] = jnp.exp2(inner * scale).astype(BF16)

    def turn(s):
        ut[s] = jnp.transpose(ubuf[s].reshape(BLOCK, PAD_C))

    r_rsx(0)
    y_rsx(0)
    for i in range(NY * NK):
        cc = (c + i) % (NY * NK)
        src = binv.at[:, :, pl.ds(pl.multiple_of(cc * PICK, PICK), PICK)]
        dst = bg.at[:, pl.ds(pl.multiple_of(c * 8, 8), 8), :]
        if i == 0:
            waits["b"] = local(src, dst)
        else:
            send("b", 0, i, src, dst, (r, cc))
    r_rsx(1)
    y_rsx(1)

    xa[0:width, :] = feat[...]

    @pl.loop(0, BLOCK // TILE)
    def _(t):
        at = pl.ds(pl.multiple_of(t * TILE, TILE), TILE)
        rows = feat[:, at].astype(F32)
        squares = jnp.sum(rows * rows, axis=0, keepdims=True)
        xa[tail_start:PAD_D, at] = with_norms(
            xa[tail_start:PAD_D, at].astype(F32), squares, tail_used, tail_used + 3, 0).astype(BF16)

    r_rsz(0)
    y_rsz(0)
    r_rsz(1)
    y_rsz(1)
    r_agz(0)
    y_agz(0)
    r_agz(1)
    y_agz(1)
    r_agx(0)
    ag2_start("y", y_block, 0)
    for i in range(1, NX):
        arrived("r_agx", 0, i)
    for i in range(1, NY * NK):
        arrived("b", 0, i)
    waits["b"].wait()
    partial_start(0, rbuf[0])
    r_agx(1)
    ag2_start("y", y_block, 1)
    ag3_start("y", y_block, 0)
    u_agz(0)
    ag3_start("y", y_block, 1)
    core_start("y", y_block, 0)
    core_end("y", 0)
    gen(0, 0, 2)
    ag2_start("u", u_block, 0)
    gen(0, 2, 4)
    ag3_start("u", u_block, 0)
    core_start("y", y_block, 1)
    gen(0, 4, 6)
    core_start("u", u_block, 0)
    gen(0, 6, 8)
    core_end("y", 1)

    second = ybuf[1, c].reshape(PICK, PAD_D)
    tail = second[:, tail_start:PAD_D].astype(F32)
    lane = lax.broadcasted_iota(jnp.int32, tail.shape, 1)
    turned = pltpu.roll(tail, 125, 1)
    tail = jnp.where((lane >= tail_used) & (lane < tail_used + 3), turned, tail)
    tail = jnp.where((lane >= tail_used + 3) & (lane < tail_used + 6), 1.0, tail)
    second = jnp.concatenate([second[:, :tail_start], tail.astype(BF16)], axis=1)
    for j in range(4):
        inner = dot_t(second, ybuf[0, 2 * j:2 * j + 2].reshape(512, PAD_D))
        k21[:, j * 512:(j + 1) * 512] = jnp.exp2(inner * scale).astype(BF16)
    for i in range(1, NX):
        arrived("r_agx", 1, i)

    core_end("u", 0)
    turn(0)
    moved = jnp.dot(k21[...], ubuf[0].reshape(BLOCK, PAD_C), preferred_element_type=F32)
    same = jnp.where(owners[0] == owners[1], 0.5, 0.0).astype(F32)
    twice = jnp.where(idxc[1] == idxr[0:1, :], same, 0.0).astype(BF16)
    moved += jnp.dot(twice, ubuf[0, c].reshape(PICK, PAD_C), preferred_element_type=F32)
    partial_start(1, rbuf[1] - moved)
    gen(1, 0, 2)
    u_agz(1)
    gen(1, 2, 4)
    ag2_start("u", u_block, 1)
    gen(1, 4, 6)
    ag3_start("u", u_block, 1)
    gen(1, 6, 8)
    core_start("u", u_block, 1)
    core_end("u", 1)

    turn(1)
    own = [jnp.where(owners[s] == r, 1.0, 0.0).astype(F32) for s in range(2)]
    mine = [ut[s, :, pl.ds(pl.multiple_of(c * PICK, PICK), PICK)] for s in range(2)]

    @pl.loop(0, BLOCK // 512)
    def _(t):
        at = pl.ds(pl.multiple_of(t * 512, 512), 512)
        change = jnp.dot(ut[0], kb[0, :, at], preferred_element_type=F32)
        change += jnp.dot(ut[1], kb[1, :, at], preferred_element_type=F32)
        added = jnp.zeros((PAD_C, 512), F32)
        for s in range(2):
            put = (picks(s, t * 512, 512) * own[s]).astype(BF16)
            added += jnp.dot(mine[s], put, preferred_element_type=F32)
        chg[:, at] = (change + 0.5 * added)[:outs, :]
        dco[:, at] = added[:outs, :]

    for copy in desc.values():
        copy.wait_send()


def per_device(features, residual, coeffs, block_inverse, block_index, owners):
    frames, width = features.shape
    outs = residual.shape[1]
    vmem = pl.BlockSpec(memory_space=pltpu.VMEM)
    change, added = pl.pallas_call(
        functools.partial(body, width, outs),
        out_shape=(jax.ShapeDtypeStruct((outs, frames), F32),
                   jax.ShapeDtypeStruct((outs, frames), F32)),
        in_specs=[pl.BlockSpec(memory_space=pltpu.SMEM)] + [vmem] * 4,
        out_specs=(vmem, vmem),
        scratch_shapes=[
            pltpu.VMEM((2, PICK, 1), jnp.int32),
            pltpu.VMEM((PAD_D, BLOCK), BF16),
            pltpu.VMEM((2, PICK, PAD_D), BF16),
            pltpu.VMEM((2, PICK, PAD_C), F32),
            pltpu.VMEM((NX, 64, PAD_C), F32),
            pltpu.VMEM((NX, 64, PAD_C), F32),
            pltpu.VMEM((2, 64, PAD_C), F32),
            pltpu.VMEM((NZ, 8, PAD_C), F32),
            pltpu.VMEM((NZ, 8, PAD_C), F32),
            pltpu.VMEM((2, 8, PAD_C), F32),
            pltpu.VMEM((2, PICK, PAD_C), F32),
            pltpu.VMEM((NX, NK, 64, 256), BF16),
            pltpu.VMEM((NX, NK, 64, 256), BF16),
            pltpu.VMEM((2, NK, 64, 256), BF16),
            pltpu.VMEM((NZ, 16, 256), BF16),
            pltpu.VMEM((NZ, 16, 256), BF16),
            pltpu.VMEM((2, 16, 256), BF16),
            pltpu.VMEM((2, 8, NX, 64, PAD_D), BF16),
            pltpu.VMEM((2, 64, PICK), F32),
            pltpu.VMEM((2, 64, PAD_C), F32),
            pltpu.VMEM((2, 8, 16, 128), F32),
            pltpu.VMEM((2, 16, 128), BF16),
            pltpu.VMEM((2, NZ, NX, NY, 16, PAD_C), BF16),
            pltpu.VMEM((2, PAD_C, BLOCK), BF16),
            pltpu.VMEM((2, BLOCK, BLOCK), BF16),
            pltpu.VMEM((PICK, BLOCK), BF16),
            pltpu.SemaphoreType.DMA((N_SEMS,)),
            pltpu.SemaphoreType.DMA((N_SEMS,)),
            pltpu.SemaphoreType.DMA((24,)),
        ],
        compiler_params=pltpu.CompilerParams(
            collective_id=0, has_side_effects=True, vmem_limit_bytes=60 * 1024 * 1024),
        name="steps",
    )(owners, features.T, residual.T, block_inverse, block_index)
    return coeffs + added.T, residual - change.T


def solution(mesh):
    both = ("rows", "cols")
    in_specs = (P(both, None), P(both, None), P(both, None), P(None, both, None),
                P(None, "cols"), P())
    out_specs = (P(both, None), P(both, None))
    return jax.shard_map(per_device, mesh=mesh, in_specs=in_specs, out_specs=out_specs,
                         check_vma=False)
```

```python
import functools
import math

import jax
import jax.numpy as jnp
from jax import lax
from jax.experimental import pallas as pl
from jax.experimental.pallas import tpu as pltpu
from jax.sharding import PartitionSpec as P

MESH = pl.DeviceIdType.MESH
NZ, NX, NY, NK = 8, 4, 4, 2
PICK = 256
BLOCK = 2048
PAD_D = 512
PAD_C = 256
TILE = 256
F32 = jnp.float32
BF16 = jnp.bfloat16

STAGES = {
    "r_rsx": 4, "r_rsz": 8, "r_agz": 8, "r_agx": 4,
    "y_rsx": 8, "y_rsz": 8, "y_agz": 8, "y_ag2": 4, "y_ag3": 16, "y_core": 16,
    "p": 8, "u_agz": 8, "u_ag2": 4, "u_ag3": 16, "u_core": 16,
}
BASE = {}
_total = 0
for _name, _count in STAGES.items():
    BASE[_name] = _total
    _total += 2 * _count
BASE["b"] = _total
N_SEMS = _total + 8


def split3(value):
    hi = value.astype(BF16)
    rest = value - hi.astype(F32)
    mid = rest.astype(BF16)
    lo = (rest - mid.astype(F32)).astype(BF16)
    return hi.astype(F32), mid.astype(F32), lo.astype(F32)


def dot_t(a, b):
    return lax.dot_general(a, b, (((1,), (1,)), ((), ())), preferred_element_type=F32)


def with_norms(tail, squares, parts_at, ones_at, axis=1):
    lane = lax.broadcasted_iota(jnp.int32, tail.shape, axis)
    hi, mid, lo = split3(-0.5 * squares)
    out = jnp.where(lane < 56, tail, 0.0)
    out = jnp.where((lane >= ones_at) & (lane < ones_at + 3), 1.0, out)
    out = jnp.where(lane == parts_at, hi, out)
    out = jnp.where(lane == parts_at + 1, mid, out)
    return jnp.where(lane == parts_at + 2, lo, out)


def body(width, outs, owners, feat, res_in, binv_in, idxr, chg, dco,
         idxc, res, binv, xa, cho, rcho, rrx0, rrx1, rsel, rrz0, rrz1, rch, rbuf, rx0, rx1, sel, rz0, rz1, ych,
         ybuf, bg, pbuf, up, uch, ubuf, ut, kb, k21, ssem, rsem, lsem):
    rrx, rrz, rx, rz = (rrx0, rrx1), (rrz0, rrz1), (rx0, rx1), (rz0, rz1)
    r = lax.axis_index("rows")
    c = lax.axis_index("cols")
    z, x = r // NX, r % NX
    y, k = c // NK, c % NK
    scale = 2.0 / width * math.log2(math.e)
    khalf = pl.ds(pl.multiple_of(k * 256, 256), 256)
    klane = pl.ds(pl.multiple_of(k * 128, 128), 128)
    tail_start = 384
    tail_used = width - tail_start

    def dev(zz, xx, yy, kk):
        return (zz * NX + xx, yy * NK + kk)

    desc = {}

    def send(name, s, i, src, dst, target):
        at = BASE[name] + (s * STAGES[name] + i if name in STAGES else i)
        copy = pltpu.make_async_remote_copy(
            src_ref=src, dst_ref=dst, send_sem=ssem.at[at], recv_sem=rsem.at[at],
            device_id=target, device_id_type=MESH)
        copy.start()
        desc[(name, s, i)] = copy

    def arrived(name, s, i):
        desc[(name, s, i)].wait_recv()

    local_count = [0]

    def local(src, dst):
        copy = pltpu.make_async_copy(src, dst, lsem.at[local_count[0]])
        local_count[0] += 1
        copy.start()
        return copy

    peers = []
    for i in range(NX):
        for kk in range(NK):
            if (i, kk) != (0, 0):
                peers.append(dev(z, (x + i) % NX, y, (k + kk) % NK))
    for i in range(1, NZ):
        peers.append(dev((z + i) % NZ, x, y, k))
    for i in range(1, NY):
        for kk in range(NK):
            peers.append(dev(z, x, (y + i) % NY, (k + kk) % NK))
    barrier = pltpu.get_barrier_semaphore()
    for peer in peers:
        pl.semaphore_signal(barrier, inc=1, device_id=peer, device_id_type=MESH)

    copies = [local(res_in, res), local(feat, xa.at[0:width, :]), local(binv_in, binv)]
    rcho[...] = jnp.zeros_like(rcho)
    diagonal = (lax.broadcasted_iota(jnp.int32, (PICK, PICK), 0)
                == lax.broadcasted_iota(jnp.int32, (PICK, PICK), 1))

    def chosen_at(s):
        index = jnp.broadcast_to(idxr[s:s + 1, :], (PICK, PICK))
        return jnp.sum(jnp.where(diagonal, index, 0).astype(F32), axis=1,
                       keepdims=True).astype(jnp.int32)

    def picks(s, start, size):
        position = lax.broadcasted_iota(jnp.int32, (PICK, size), 1) + start
        return jnp.where(idxc[s] == position, 1.0, 0.0)

    def choose_res(s):
        idxc[s] = chosen_at(s)
        pick = picks(s, 0, BLOCK).astype(BF16)
        res_hi = res[...].astype(BF16)
        res_lo = (res[...] - res_hi.astype(F32)).astype(BF16)
        rcho[s, :, 0:outs] = dot_t(pick, res_hi) + dot_t(pick, res_lo)

    def choose_feat(s):
        pick = picks(s, 0, BLOCK).astype(BF16)
        rows = dot_t(pick, xa[0:width, :])
        squares = jnp.sum(rows * rows, axis=1, keepdims=True)
        cho[s, :, 0:width] = rows.astype(BF16)
        cho[s, :, tail_start:PAD_D] = with_norms(
            cho[s, :, tail_start:PAD_D].astype(F32), squares, tail_used + 3, tail_used).astype(BF16)

    copies[0].wait()
    choose_res(0)
    pl.semaphore_wait(barrier, len(peers))

    waits = {}

    def r_rsx(s):
        for i in range(1, NX):
            xx = (x + i) % NX
            send("r_rsx", s, i, rcho.at[s, pl.ds(pl.multiple_of(xx * 64, 64), 64), :],
                 rrx[s].at[x], dev(z, xx, y, k))
        waits[("r_rsx", s)] = local(
            rcho.at[s, pl.ds(pl.multiple_of(x * 64, 64), 64), :], rrx[s].at[x])

    def y_rsx(s):
        for i in range(NX):
            xx = (x + i) % NX
            for kk in range(NK):
                if (i, kk) == (0, 0):
                    continue
                k2 = (k + kk) % NK
                send("y_rsx", s, i * NK + kk,
                     cho.at[s, pl.ds(pl.multiple_of(xx * 64, 64), 64),
                            pl.ds(pl.multiple_of(k2 * 256, 256), 256)],
                     rx[s].at[x, k], dev(z, xx, y, k2))
        waits[("y_rsx", s)] = local(
            cho.at[s, pl.ds(pl.multiple_of(x * 64, 64), 64), khalf], rx[s].at[x, k])

    def r_rsz(s):
        for i in range(1, NX):
            arrived("r_rsx", s, i)
        waits[("r_rsx", s)].wait()
        rsel[s] = rrx[s][owners[s] % NX]
        for i in range(NZ):
            zz = (z + i) % NZ
            src = rsel.at[s, pl.ds(pl.multiple_of(zz * 8, 8), 8), :]
            if i == 0:
                waits[("r_rsz", s)] = local(src, rrz[s].at[z])
            else:
                send("r_rsz", s, i, src, rrz[s].at[z], dev(zz, x, y, k))

    def y_rsz(s):
        for i in range(NX):
            for kk in range(NK):
                if (i, kk) != (0, 0):
                    arrived("y_rsx", s, i * NK + kk)
        waits[("y_rsx", s)].wait()
        sel[s] = rx[s][owners[s] % NX]
        for i in range(NZ):
            zz = (z + i) % NZ
            src = sel.at[s, zz // 4, pl.ds(pl.multiple_of((zz % 4) * 16, 16), 16), :]
            if i == 0:
                waits[("y_rsz", s)] = local(src, rz[s].at[z])
            else:
                send("y_rsz", s, i, src, rz[s].at[z], dev(zz, x, y, k))

    def r_agz(s):
        for i in range(1, NZ):
            arrived("r_rsz", s, i)
        waits[("r_rsz", s)].wait()
        rch[s] = rrz[s][owners[s] // NX]
        place = rbuf.at[s, pl.ds(pl.multiple_of(x * 64 + z * 8, 8), 8), :]
        for i in range(1, NZ):
            send("r_agz", s, i, rch.at[s], place, dev((z + i) % NZ, x, y, k))
        waits[("r_agz", s)] = local(rch.at[s], place)

    def y_agz(s):
        for i in range(1, NZ):
            arrived("y_rsz", s, i)
        waits[("y_rsz", s)].wait()
        ych[s] = rz[s][owners[s] // NX]
        place = ybuf.at[s, 2 * y + z // 4, x,
                        pl.ds(pl.multiple_of((z % 4) * 16, 16), 16), khalf]
        for i in range(1, NZ):
            send("y_agz", s, i, ych.at[s], place, dev((z + i) % NZ, x, y, k))
        waits[("y_agz", s)] = local(ych.at[s], place)

    def r_agx(s):
        for i in range(1, NZ):
            arrived("r_agz", s, i)
        waits[("r_agz", s)].wait()
        part = rbuf.at[s, pl.ds(pl.multiple_of(x * 64, 64), 64), :]
        for i in range(1, NX):
            send("r_agx", s, i, part, part, dev(z, (x + i) % NX, y, k))

    g = (1 - k) * x + k * y
    q = (1 - k) * y + k * x

    def y_block(s, gg, qq):
        bx = (1 - k) * gg + k * qq
        by = k * gg + (1 - k) * qq
        return ybuf.at[s, pl.ds(2 * by, 2), bx, :, khalf]

    def u_block(s, gg, qq):
        bx = (1 - k) * gg + k * qq
        by = k * gg + (1 - k) * qq
        return ubuf.at[s, :, bx, by, :, klane]

    def to_second(i):
        return dev(z, (x + i * (1 - k)) % NX, (y + i * k) % NY, k)

    def to_third(i):
        return dev(z, (x + i * k) % NX, (y + i * (1 - k)) % NY, k)

    def to_core(kind, block, s, d, i):
        part = block(s, (g - d + NX) % NX, (q - i + NY) % NY)
        send(kind + "_core", s, d * 4 + i, part, part, dev(z, x, y, 1 - k))

    def ring_send(kind, block, s, d):
        part = block(s, (g - d + NX) % NX, q)
        for i in (1, 3):
            send(kind + "_ag3", s, d * 4 + i, part, part, to_third(i))
        to_core(kind, block, s, d, 0)

    def ring_pass(kind, block, s, d):
        for i, slot, half in ((1, 2, 0), (3, 0, 1)):
            arrived(kind + "_ag3", s, d * 4 + i)
            part = half_of(kind, block(s, (g - d + NX) % NX, (q - i + NY) % NY), half)
            send(kind + "_ag3", s, d * 4 + slot, part, part, to_third(i))
            to_core(kind, block, s, d, i)

    def half_of(kind, ref, half):
        if kind == "y":
            return ref.at[half:half + 1]
        return ref.at[half * 4:half * 4 + 4]

    def ag2_start(kind, block, s):
        for i in range(1, NZ):
            arrived(kind + "_agz", s, i)
        waits[(kind + "_agz", s)].wait()
        part = block(s, g, q)
        for i in range(1, NX):
            send(kind + "_ag2", s, i, part, part, to_second(i))
        ring_send(kind, block, s, 0)

    def ag3_start(kind, block, s):
        for d in range(1, NX):
            arrived(kind + "_ag2", s, d)
            ring_send(kind, block, s, d)

    def pass_start(kind, block, s):
        for d in range(NX):
            ring_pass(kind, block, s, d)

    def core_start(kind, block, s):
        for d in range(NX):
            arrived(kind + "_ag3", s, d * 4 + 2)
            arrived(kind + "_ag3", s, d * 4)
            to_core(kind, block, s, d, 2)

    def core_end(kind, s):
        for d in range(NX):
            for i in range(NY):
                arrived(kind + "_core", s, d * 4 + i)

    def partial_start(s, values):
        pbuf[s] = jnp.dot(bg[s], values, precision=lax.Precision.HIGHEST,
                          preferred_element_type=F32)
        for i in range(NY * NK):
            cc = (c + i) % (NY * NK)
            src = pbuf.at[s, pl.ds(pl.multiple_of((cc // NK) * 16, 16), 16),
                          pl.ds(pl.multiple_of((cc % NK) * 128, 128), 128)]
            if i == 0:
                waits[("p", s)] = local(src, up.at[s, c])
            else:
                send("p", s, i, src, up.at[s, c], (r, cc))

    def u_agz(s):
        for i in range(1, NY * NK):
            arrived("p", s, i)
        waits[("p", s)].wait()
        uch[s] = jnp.sum(up[s], axis=0).astype(BF16)
        place = ubuf.at[s, z, x, y, :, klane]
        for i in range(1, NZ):
            send("u_agz", s, i, uch.at[s], place, dev((z + i) % NZ, x, y, k))
        waits[("u_agz", s)] = local(uch.at[s], place)

    def gen(s, first, last):
        @pl.loop(first, last)
        def _(t):
            at = pl.ds(pl.multiple_of(t * TILE, TILE), TILE)
            points = ybuf[s, t].reshape(TILE, PAD_D)
            for j in range(4):
                inner = jnp.dot(points, xa[:, j * 512:(j + 1) * 512], preferred_element_type=F32)
                kb[s, at, j * 512:(j + 1) * 512] = jnp.exp2(inner * scale).astype(BF16)

    def turn(s):
        ut[s] = jnp.transpose(ubuf[s].reshape(BLOCK, PAD_C))

    r_rsx(0)
    copies[2].wait()
    for i in range(NY * NK):
        cc = (c + i) % (NY * NK)
        src = binv.at[:, :, pl.ds(pl.multiple_of(cc * PICK, PICK), PICK)]
        dst = bg.at[:, pl.ds(pl.multiple_of(c * 8, 8), 8), :]
        if i == 0:
            waits["b"] = local(src, dst)
        else:
            send("b", 0, i, src, dst, (r, cc))
    copies[1].wait()
    choose_feat(0)
    r_rsz(0)
    y_rsx(0)
    choose_res(1)
    choose_feat(1)
    r_agz(0)
    y_rsz(0)
    y_rsx(1)

    @pl.loop(0, BLOCK // TILE)
    def _(t):
        at = pl.ds(pl.multiple_of(t * TILE, TILE), TILE)
        rows = xa[0:width, at].astype(F32)
        squares = jnp.sum(rows * rows, axis=0, keepdims=True)
        xa[tail_start:PAD_D, at] = with_norms(
            xa[tail_start:PAD_D, at].astype(F32), squares, tail_used, tail_used + 3, 0).astype(BF16)

    r_agx(0)
    y_agz(0)
    r_rsx(1)
    for i in range(1, NX):
        arrived("r_agx", 0, i)
    for i in range(1, NY * NK):
        arrived("b", 0, i)
    waits["b"].wait()
    partial_start(0, rbuf[0])
    ag2_start("y", y_block, 0)
    y_rsz(1)
    u_agz(0)
    ag3_start("y", y_block, 0)
    r_rsz(1)
    y_agz(1)
    ag2_start("u", u_block, 0)
    pass_start("y", y_block, 0)
    r_agz(1)
    ag3_start("u", u_block, 0)
    core_start("y", y_block, 0)
    ag2_start("y", y_block, 1)
    pass_start("u", u_block, 0)
    core_end("y", 0)
    r_agx(1)
    gen(0, 0, 2)
    core_start("u", u_block, 0)
    ag3_start("y", y_block, 1)
    gen(0, 2, 4)
    pass_start("y", y_block, 1)
    gen(0, 4, 6)
    core_start("y", y_block, 1)
    gen(0, 6, 8)
    core_end("y", 1)

    second = ybuf[1, c].reshape(PICK, PAD_D)
    tail = second[:, tail_start:PAD_D].astype(F32)
    lane = lax.broadcasted_iota(jnp.int32, tail.shape, 1)
    turned = pltpu.roll(tail, 125, 1)
    tail = jnp.where((lane >= tail_used) & (lane < tail_used + 3), turned, tail)
    tail = jnp.where((lane >= tail_used + 3) & (lane < tail_used + 6), 1.0, tail)
    second = jnp.concatenate([second[:, :tail_start], tail.astype(BF16)], axis=1)
    for j in range(4):
        inner = dot_t(second, ybuf[0, 2 * j:2 * j + 2].reshape(512, PAD_D))
        k21[:, j * 512:(j + 1) * 512] = jnp.exp2(inner * scale).astype(BF16)
    for i in range(1, NX):
        arrived("r_agx", 1, i)

    core_end("u", 0)
    turn(0)
    moved = jnp.dot(k21[...], ubuf[0].reshape(BLOCK, PAD_C), preferred_element_type=F32)
    same = jnp.where(owners[0] == owners[1], 0.5, 0.0).astype(F32)
    twice = jnp.where(idxc[1] == idxr[0:1, :], same, 0.0).astype(BF16)
    moved += jnp.dot(twice, ubuf[0, c].reshape(PICK, PAD_C), preferred_element_type=F32)
    partial_start(1, rbuf[1] - moved)
    gen(1, 0, 2)
    u_agz(1)
    gen(1, 2, 4)
    ag2_start("u", u_block, 1)
    gen(1, 4, 6)
    ag3_start("u", u_block, 1)
    gen(1, 6, 8)
    pass_start("u", u_block, 1)
    core_start("u", u_block, 1)
    core_end("u", 1)

    turn(1)
    own = [jnp.where(owners[s] == r, 1.0, 0.0).astype(F32) for s in range(2)]
    mine = [ut[s, :, pl.ds(pl.multiple_of(c * PICK, PICK), PICK)] for s in range(2)]

    @pl.loop(0, BLOCK // 512)
    def _(t):
        at = pl.ds(pl.multiple_of(t * 512, 512), 512)
        change = jnp.dot(ut[0], kb[0, :, at], preferred_element_type=F32)
        change += jnp.dot(ut[1], kb[1, :, at], preferred_element_type=F32)
        added = jnp.zeros((PAD_C, 512), F32)
        for s in range(2):
            put = (picks(s, t * 512, 512) * own[s]).astype(BF16)
            added += jnp.dot(mine[s], put, preferred_element_type=F32)
        chg[:, at] = (change + 0.5 * added)[:outs, :]
        dco[:, at] = added[:outs, :]

    for copy in desc.values():
        copy.wait_send()


def per_device(features, residual, coeffs, block_inverse, block_index, owners):
    frames, width = features.shape
    outs = residual.shape[1]
    vmem = pl.BlockSpec(memory_space=pltpu.VMEM)
    change, added = pl.pallas_call(
        functools.partial(body, width, outs),
        out_shape=(jax.ShapeDtypeStruct((outs, frames), F32),
                   jax.ShapeDtypeStruct((outs, frames), F32)),
        in_specs=[pl.BlockSpec(memory_space=pltpu.SMEM)] + [pl.BlockSpec(memory_space=pl.ANY)] * 3 + [vmem],
        out_specs=(vmem, vmem),
        scratch_shapes=[
            pltpu.VMEM((2, PICK, 1), jnp.int32),
            pltpu.VMEM((outs, BLOCK), F32),
            pltpu.VMEM((2, 8, BLOCK), F32),
            pltpu.VMEM((PAD_D, BLOCK), BF16),
            pltpu.VMEM((2, PICK, PAD_D), BF16),
            pltpu.VMEM((2, PICK, PAD_C), F32),
            pltpu.VMEM((NX, 64, PAD_C), F32),
            pltpu.VMEM((NX, 64, PAD_C), F32),
            pltpu.VMEM((2, 64, PAD_C), F32),
            pltpu.VMEM((NZ, 8, PAD_C), F32),
            pltpu.VMEM((NZ, 8, PAD_C), F32),
            pltpu.VMEM((2, 8, PAD_C), F32),
            pltpu.VMEM((2, PICK, PAD_C), F32),
            pltpu.VMEM((NX, NK, 64, 256), BF16),
            pltpu.VMEM((NX, NK, 64, 256), BF16),
            pltpu.VMEM((2, NK, 64, 256), BF16),
            pltpu.VMEM((NZ, 16, 256), BF16),
            pltpu.VMEM((NZ, 16, 256), BF16),
            pltpu.VMEM((2, 16, 256), BF16),
            pltpu.VMEM((2, 8, NX, 64, PAD_D), BF16),
            pltpu.VMEM((2, 64, PICK), F32),
            pltpu.VMEM((2, 64, PAD_C), F32),
            pltpu.VMEM((2, 8, 16, 128), F32),
            pltpu.VMEM((2, 16, 128), BF16),
            pltpu.VMEM((2, NZ, NX, NY, 16, PAD_C), BF16),
            pltpu.VMEM((2, PAD_C, BLOCK), BF16),
            pltpu.VMEM((2, BLOCK, BLOCK), BF16),
            pltpu.VMEM((PICK, BLOCK), BF16),
            pltpu.SemaphoreType.DMA((N_SEMS,)),
            pltpu.SemaphoreType.DMA((N_SEMS,)),
            pltpu.SemaphoreType.DMA((24,)),
        ],
        compiler_params=pltpu.CompilerParams(
            collective_id=0, has_side_effects=True, vmem_limit_bytes=60 * 1024 * 1024),
        name="steps",
    )(owners, features.T, residual.T, block_inverse, block_index)
    return coeffs + added.T, residual - change.T


def solution(mesh):
    both = ("rows", "cols")
    in_specs = (P(both, None), P(both, None), P(both, None), P(None, both, None),
                P(None, "cols"), P())
    out_specs = (P(both, None), P(both, None))
    return jax.shard_map(per_device, mesh=mesh, in_specs=in_specs, out_specs=out_specs,
                         check_vma=False)
```

```python
import functools
import math

import jax
import jax.numpy as jnp
from jax import lax
from jax.experimental import pallas as pl
from jax.experimental.pallas import tpu as pltpu
from jax.sharding import PartitionSpec as P

MESH = pl.DeviceIdType.MESH
NZ, NX, NY, NK = 8, 4, 4, 2
PICK = 256
BLOCK = 2048
PAD_D = 512
PAD_C = 256
PAD_R = 160
TILE = 256
F32 = jnp.float32
BF16 = jnp.bfloat16

STAGES = {
    "r_rsx": 4, "r_rsz": 8, "r_agz": 8, "r_agx": 4,
    "y_rsx": 8, "y_rsz": 8, "y_agz": 8, "y_ag2": 4, "y_ag3": 16, "y_core": 16,
    "p": 8, "u_agz": 8, "u_ag2": 4, "u_ag3": 16, "u_core": 16,
}
BASE = {}
_total = 0
for _name, _count in STAGES.items():
    BASE[_name] = _total
    _total += 2 * _count
BASE["b"] = _total
N_SEMS = _total + 8


def split3(value):
    hi = value.astype(BF16)
    rest = value - hi.astype(F32)
    mid = rest.astype(BF16)
    lo = (rest - mid.astype(F32)).astype(BF16)
    return hi.astype(F32), mid.astype(F32), lo.astype(F32)


def dot_t(a, b):
    return lax.dot_general(a, b, (((1,), (1,)), ((), ())), preferred_element_type=F32)


def with_norms(tail, squares, parts_at, ones_at, axis=1):
    lane = lax.broadcasted_iota(jnp.int32, tail.shape, axis)
    hi, mid, lo = split3(-0.5 * squares)
    out = jnp.where(lane < 56, tail, 0.0)
    out = jnp.where((lane >= ones_at) & (lane < ones_at + 3), 1.0, out)
    out = jnp.where(lane == parts_at, hi, out)
    out = jnp.where(lane == parts_at + 1, mid, out)
    return jnp.where(lane == parts_at + 2, lo, out)


def body(width, outs, owners, feat, res_in, co_in, binv_in, idxr, new_co, new_res,
         idxc, res, co, binv, xa, cho, rcho, rrx0, rrx1, rsel, rrz0, rrz1, rch, rbuf, rx0, rx1, sel, rz0, rz1, ych,
         ybuf, bg, pbuf, up, uch, ubuf, ut, kb, k21, ssem, rsem, lsem):
    rrx, rrz, rx, rz = (rrx0, rrx1), (rrz0, rrz1), (rx0, rx1), (rz0, rz1)
    r = lax.axis_index("rows")
    c = lax.axis_index("cols")
    z, x = r // NX, r % NX
    y, k = c // NK, c % NK
    scale = 2.0 / width * math.log2(math.e)
    khalf = pl.ds(pl.multiple_of(k * 256, 256), 256)
    klane = pl.ds(pl.multiple_of(k * 128, 128), 128)
    tail_start = 384
    tail_used = width - tail_start

    def dev(zz, xx, yy, kk):
        return (zz * NX + xx, yy * NK + kk)

    desc = {}
    sent = []

    def when(need, action):
        if need is None:
            action()
        else:
            pl.when(need)(action)

    def send(name, s, i, src, dst, target, need=None):
        at = BASE[name] + (s * STAGES[name] + i if name in STAGES else i)
        copy = pltpu.make_async_remote_copy(
            src_ref=src, dst_ref=dst, send_sem=ssem.at[at], recv_sem=rsem.at[at],
            device_id=target, device_id_type=MESH)
        when(need, copy.start)
        desc[(name, s, i)] = copy
        sent.append((copy, need))

    def arrived(name, s, i, need=None):
        when(need, desc[(name, s, i)].wait_recv)

    def sends_done():
        for copy, need in sent:
            when(need, copy.wait_send)
        sent.clear()

    local_count = [0]

    def local(src, dst, need=None):
        copy = pltpu.make_async_copy(src, dst, lsem.at[local_count[0]])
        local_count[0] += 1
        when(need, copy.start)
        return copy

    peers = []
    for i in range(NX):
        for kk in range(NK):
            if (i, kk) != (0, 0):
                peers.append(dev(z, (x + i) % NX, y, (k + kk) % NK))
    for i in range(1, NZ):
        peers.append(dev((z + i) % NZ, x, y, k))
    for i in range(1, NY):
        for kk in range(NK):
            peers.append(dev(z, x, (y + i) % NY, (k + kk) % NK))
    barrier = pltpu.get_barrier_semaphore()
    for peer in peers:
        pl.semaphore_signal(barrier, inc=1, device_id=peer, device_id_type=MESH)

    copies = [local(res_in, res), local(feat, xa.at[0:width, :]), local(binv_in, binv),
              local(co_in, co)]
    rcho[...] = jnp.zeros_like(rcho)
    pbuf[...] = jnp.zeros_like(pbuf)
    diagonal = (lax.broadcasted_iota(jnp.int32, (PICK, PICK), 0)
                == lax.broadcasted_iota(jnp.int32, (PICK, PICK), 1))

    def chosen_at(s):
        index = jnp.broadcast_to(idxr[s:s + 1, :], (PICK, PICK))
        return jnp.sum(jnp.where(diagonal, index, 0).astype(F32), axis=1,
                       keepdims=True).astype(jnp.int32)

    def picks(s, start, size):
        position = lax.broadcasted_iota(jnp.int32, (PICK, size), 1) + start
        return jnp.where(idxc[s] == position, 1.0, 0.0)

    def choose_res(s):
        pick = picks(s, 0, BLOCK).astype(BF16)
        res_hi = res[...].astype(BF16)
        res_lo = (res[...] - res_hi.astype(F32)).astype(BF16)
        rcho[s, 0:outs, :] = dot_t(res_hi, pick) + dot_t(res_lo, pick)

    def choose_feat(s):
        pick = picks(s, 0, BLOCK).astype(BF16)
        rows = dot_t(pick, xa[0:width, :])
        squares = jnp.sum(rows * rows, axis=1, keepdims=True)
        cho[s, :, 0:width] = rows.astype(BF16)
        cho[s, :, tail_start:PAD_D] = with_norms(
            cho[s, :, tail_start:PAD_D].astype(F32), squares, tail_used + 3, tail_used).astype(BF16)

    for s in range(2):
        idxc[s] = chosen_at(s)
    copies[0].wait()
    choose_res(0)
    pl.semaphore_wait(barrier, len(peers))

    waits = {}

    def r_rsx(s):
        for i in range(1, NX):
            xx = (x + i) % NX
            send("r_rsx", s, i, rcho.at[s, pl.ds(pl.multiple_of(xx * 40, 8), 40), :],
                 rrx[s].at[x], dev(z, xx, y, k))
        waits[("r_rsx", s)] = local(
            rcho.at[s, pl.ds(pl.multiple_of(x * 40, 8), 40), :], rrx[s].at[x])

    def y_rsx(s):
        for i in range(NX):
            xx = (x + i) % NX
            for kk in range(NK):
                if (i, kk) == (0, 0):
                    continue
                k2 = (k + kk) % NK
                send("y_rsx", s, i * NK + kk,
                     cho.at[s, pl.ds(pl.multiple_of(xx * 64, 64), 64),
                            pl.ds(pl.multiple_of(k2 * 256, 256), 256)],
                     rx[s].at[x, k], dev(z, xx, y, k2))
        waits[("y_rsx", s)] = local(
            cho.at[s, pl.ds(pl.multiple_of(x * 64, 64), 64), khalf], rx[s].at[x, k])

    def r_rsz(s):
        for i in range(1, NX):
            arrived("r_rsx", s, i)
        waits[("r_rsx", s)].wait()
        rsel[s] = rrx[s][owners[s] % NX]
        for i in range(NZ):
            zz = (z + i) % NZ
            row = zz % 5
            src = rsel.at[s, pl.ds(pl.multiple_of(row * 8, 8), 8), :]
            if i == 0:
                waits[("r_rsz", s)] = local(src, rrz[s].at[z], zz < 5)
            else:
                send("r_rsz", s, i, src, rrz[s].at[z], dev(zz, x, y, k), zz < 5)

    def y_rsz(s):
        for i in range(NX):
            for kk in range(NK):
                if (i, kk) != (0, 0):
                    arrived("y_rsx", s, i * NK + kk)
        waits[("y_rsx", s)].wait()
        sel[s] = rx[s][owners[s] % NX]
        for i in range(NZ):
            zz = (z + i) % NZ
            src = sel.at[s, zz // 4, pl.ds(pl.multiple_of((zz % 4) * 16, 16), 16), :]
            if i == 0:
                waits[("y_rsz", s)] = local(src, rz[s].at[z])
            else:
                send("y_rsz", s, i, src, rz[s].at[z], dev(zz, x, y, k))

    def r_agz(s):
        place = rbuf.at[s, pl.ds(pl.multiple_of(x * 40 + (z % 5) * 8, 8), 8), :]
        for i in range(1, NZ):
            arrived("r_rsz", s, i, z < 5)

        @pl.when(z < 5)
        def _():
            waits[("r_rsz", s)].wait()
            rch[s] = rrz[s][owners[s] // NX]

        for i in range(1, NZ):
            send("r_agz", s, i, rch.at[s], place, dev((z + i) % NZ, x, y, k), z < 5)
        waits[("r_agz", s)] = local(rch.at[s], place, z < 5)

    def y_agz(s):
        for i in range(1, NZ):
            arrived("y_rsz", s, i)
        waits[("y_rsz", s)].wait()
        ych[s] = rz[s][owners[s] // NX]
        place = ybuf.at[s, 2 * y + z // 4, x,
                        pl.ds(pl.multiple_of((z % 4) * 16, 16), 16), khalf]
        for i in range(1, NZ):
            send("y_agz", s, i, ych.at[s], place, dev((z + i) % NZ, x, y, k))
        waits[("y_agz", s)] = local(ych.at[s], place)

    def r_agx(s):
        for i in range(1, NZ):
            arrived("r_agz", s, i, (z - i + NZ) % NZ < 5)
        when(z < 5, waits[("r_agz", s)].wait)
        part = rbuf.at[s, pl.ds(pl.multiple_of(x * 40, 8), 40), :]
        for i in range(1, NX):
            send("r_agx", s, i, part, part, dev(z, (x + i) % NX, y, k))

    g = (1 - k) * x + k * y
    q = (1 - k) * y + k * x

    def y_block(s, gg, qq):
        bx = (1 - k) * gg + k * qq
        by = k * gg + (1 - k) * qq
        return ybuf.at[s, pl.ds(2 * by, 2), bx, :, khalf]

    def u_block(s, gg, qq):
        bx = (1 - k) * gg + k * qq
        by = k * gg + (1 - k) * qq
        return ubuf.at[s, :, bx, by, :, klane]

    def to_second(i):
        return dev(z, (x + i * (1 - k)) % NX, (y + i * k) % NY, k)

    def to_third(i):
        return dev(z, (x + i * k) % NX, (y + i * (1 - k)) % NY, k)

    def to_core(kind, block, s, d, i):
        part = block(s, (g - d + NX) % NX, (q - i + NY) % NY)
        send(kind + "_core", s, d * 4 + i, part, part, dev(z, x, y, 1 - k))

    def ring_send(kind, block, s, d):
        part = block(s, (g - d + NX) % NX, q)
        for i in (1, 3):
            send(kind + "_ag3", s, d * 4 + i, part, part, to_third(i))
        to_core(kind, block, s, d, 0)

    def ring_pass(kind, block, s, d):
        for i, slot, half in ((1, 2, 0), (3, 0, 1)):
            arrived(kind + "_ag3", s, d * 4 + i)
            part = half_of(kind, block(s, (g - d + NX) % NX, (q - i + NY) % NY), half)
            send(kind + "_ag3", s, d * 4 + slot, part, part, to_third(i))
            to_core(kind, block, s, d, i)

    def half_of(kind, ref, half):
        if kind == "y":
            return ref.at[half:half + 1]
        return ref.at[half * 4:half * 4 + 4]

    def ag2_start(kind, block, s):
        for i in range(1, NZ):
            arrived(kind + "_agz", s, i)
        waits[(kind + "_agz", s)].wait()
        part = block(s, g, q)
        for i in range(1, NX):
            send(kind + "_ag2", s, i, part, part, to_second(i))
        ring_send(kind, block, s, 0)

    def ag3_start(kind, block, s):
        for d in range(1, NX):
            arrived(kind + "_ag2", s, d)
            ring_send(kind, block, s, d)

    def pass_start(kind, block, s):
        for d in range(NX):
            ring_pass(kind, block, s, d)

    def core_start(kind, block, s):
        for d in range(NX):
            arrived(kind + "_ag3", s, d * 4 + 2)
            arrived(kind + "_ag3", s, d * 4)
            to_core(kind, block, s, d, 2)

    def core_end(kind, s):
        for d in range(NX):
            for i in range(NY):
                arrived(kind + "_core", s, d * 4 + i)

    def partial_start(s, values):
        pbuf[s, :, 0:PAD_R] = lax.dot_general(
            bg[s], values, (((1,), (1,)), ((), ())), precision=lax.Precision.HIGHEST,
            preferred_element_type=F32)
        for i in range(NY * NK):
            cc = (c + i) % (NY * NK)
            src = pbuf.at[s, pl.ds(pl.multiple_of((cc // NK) * 16, 16), 16),
                          pl.ds(pl.multiple_of((cc % NK) * 128, 128), 128)]
            if i == 0:
                waits[("p", s)] = local(src, up.at[s, c])
            else:
                send("p", s, i, src, up.at[s, c], (r, cc))

    def u_agz(s):
        for i in range(1, NY * NK):
            arrived("p", s, i)
        waits[("p", s)].wait()
        uch[s] = jnp.sum(up[s], axis=0).astype(BF16)
        place = ubuf.at[s, z, x, y, :, klane]
        for i in range(1, NZ):
            send("u_agz", s, i, uch.at[s], place, dev((z + i) % NZ, x, y, k))
        waits[("u_agz", s)] = local(uch.at[s], place)

    def gen(s, first, last):
        @pl.loop(first, last)
        def _(t):
            at = pl.ds(pl.multiple_of(t * TILE, TILE), TILE)
            points = ybuf[s, t].reshape(TILE, PAD_D)
            for j in range(4):
                inner = jnp.dot(points, xa[:, j * 512:(j + 1) * 512], preferred_element_type=F32)
                kb[s, at, j * 512:(j + 1) * 512] = jnp.exp2(inner * scale).astype(BF16)

    def turn(s):
        ut[s] = jnp.transpose(ubuf[s].reshape(BLOCK, PAD_C))

    r_rsx(0)
    copies[2].wait()
    for i in range(NY * NK):
        cc = (c + i) % (NY * NK)
        src = binv.at[:, :, pl.ds(pl.multiple_of(cc * PICK, PICK), PICK)]
        dst = bg.at[:, pl.ds(pl.multiple_of(c * 8, 8), 8), :]
        if i == 0:
            waits["b"] = local(src, dst)
        else:
            send("b", 0, i, src, dst, (r, cc))
    copies[1].wait()
    choose_feat(0)
    r_rsz(0)
    y_rsx(0)
    choose_feat(1)
    y_rsx(1)
    choose_res(1)
    r_agz(0)
    y_rsz(0)

    @pl.loop(0, BLOCK // TILE)
    def _(t):
        at = pl.ds(pl.multiple_of(t * TILE, TILE), TILE)
        rows = xa[0:width, at].astype(F32)
        squares = jnp.sum(rows * rows, axis=0, keepdims=True)
        xa[tail_start:PAD_D, at] = with_norms(
            xa[tail_start:PAD_D, at].astype(F32), squares, tail_used, tail_used + 3, 0).astype(BF16)

    r_agx(0)
    y_rsz(1)
    r_rsx(1)
    y_agz(0)
    for i in range(1, NX):
        arrived("r_agx", 0, i)
    for i in range(1, NY * NK):
        arrived("b", 0, i)
    waits["b"].wait()
    partial_start(0, rbuf[0])
    y_agz(1)
    r_rsz(1)
    ag2_start("y", y_block, 0)
    u_agz(0)
    ag2_start("y", y_block, 1)
    ag3_start("y", y_block, 0)
    r_agz(1)
    ag2_start("u", u_block, 0)
    ag3_start("y", y_block, 1)
    pass_start("y", y_block, 0)
    ag3_start("u", u_block, 0)
    r_agx(1)
    pass_start("y", y_block, 1)
    pass_start("u", u_block, 0)
    core_start("y", y_block, 0)
    core_start("y", y_block, 1)
    core_start("u", u_block, 0)
    core_end("y", 0)
    core_end("y", 1)

    second = ybuf[1, c].reshape(PICK, PAD_D)
    tail = second[:, tail_start:PAD_D].astype(F32)
    lane = lax.broadcasted_iota(jnp.int32, tail.shape, 1)
    turned = pltpu.roll(tail, 125, 1)
    tail = jnp.where((lane >= tail_used) & (lane < tail_used + 3), turned, tail)
    tail = jnp.where((lane >= tail_used + 3) & (lane < tail_used + 6), 1.0, tail)
    second = jnp.concatenate([second[:, :tail_start], tail.astype(BF16)], axis=1)
    for j in range(4):
        inner = dot_t(second, ybuf[0, 2 * j:2 * j + 2].reshape(512, PAD_D))
        k21[:, j * 512:(j + 1) * 512] = jnp.exp2(inner * scale).astype(BF16)
    for i in range(1, NX):
        arrived("r_agx", 1, i)

    same = jnp.where(owners[0] == owners[1], 0.5, 0.0).astype(F32)
    twice = jnp.where(idxc[1] == idxr[0:1, :], same, 0.0).astype(BF16)
    core_end("u", 0)
    turn(0)
    mine = pl.ds(pl.multiple_of(c * PICK, PICK), PICK)
    moved = dot_t(ut[0, 0:PAD_R, :], k21[...])
    moved += dot_t(ut[0, 0:PAD_R, mine], twice)
    partial_start(1, rbuf[1] - moved)

    def product(s, t, from_res, from_co):
        at = pl.ds(pl.multiple_of(t * 512, 512), 512)
        change = jnp.dot(ut[s], kb[s, :, at], preferred_element_type=F32)
        own = jnp.where(owners[s] == r, 1.0, 0.0).astype(F32)
        put = (picks(s, t * 512, 512) * own).astype(BF16)
        added = jnp.dot(ut[s, :, mine], put, preferred_element_type=F32)
        new_res[:, at] = from_res[:, at] - (change + 0.5 * added)[:outs, :]
        new_co[:, at] = from_co[:, at] + added[:outs, :]

    gen(0, 0, 4)
    u_agz(1)
    gen(0, 4, 8)
    copies[3].wait()
    ag2_start("u", u_block, 1)

    @pl.loop(0, 4)
    def _(t):
        product(0, t, res, co)

    ag3_start("u", u_block, 1)
    gen(1, 0, 4)
    pass_start("u", u_block, 1)
    gen(1, 4, 8)
    core_start("u", u_block, 1)
    sends_done()
    core_end("u", 1)
    turn(1)

    @pl.loop(0, 4)
    def _(t):
        product(1, t, new_res, new_co)


def per_device(features, residual, coeffs, block_inverse, block_index, owners):
    frames, width = features.shape
    outs = residual.shape[1]
    vmem = pl.BlockSpec(memory_space=pltpu.VMEM)
    new_coeffs, new_residual = pl.pallas_call(
        functools.partial(body, width, outs),
        out_shape=(jax.ShapeDtypeStruct((outs, frames), F32),
                   jax.ShapeDtypeStruct((outs, frames), F32)),
        in_specs=[pl.BlockSpec(memory_space=pltpu.SMEM)] + [pl.BlockSpec(memory_space=pl.ANY)] * 4 + [vmem],
        out_specs=(vmem, vmem),
        scratch_shapes=[
            pltpu.VMEM((2, PICK, 1), jnp.int32),
            pltpu.VMEM((outs, BLOCK), F32),
            pltpu.VMEM((outs, BLOCK), F32),
            pltpu.VMEM((2, 8, BLOCK), F32),
            pltpu.VMEM((PAD_D, BLOCK), BF16),
            pltpu.VMEM((2, PICK, PAD_D), BF16),
            pltpu.VMEM((2, PAD_R, PICK), F32),
            pltpu.VMEM((NX, 40, PICK), F32),
            pltpu.VMEM((NX, 40, PICK), F32),
            pltpu.VMEM((2, 40, PICK), F32),
            pltpu.VMEM((NZ, 8, PICK), F32),
            pltpu.VMEM((NZ, 8, PICK), F32),
            pltpu.VMEM((2, 8, PICK), F32),
            pltpu.VMEM((2, PAD_R, PICK), F32),
            pltpu.VMEM((NX, NK, 64, 256), BF16),
            pltpu.VMEM((NX, NK, 64, 256), BF16),
            pltpu.VMEM((2, NK, 64, 256), BF16),
            pltpu.VMEM((NZ, 16, 256), BF16),
            pltpu.VMEM((NZ, 16, 256), BF16),
            pltpu.VMEM((2, 16, 256), BF16),
            pltpu.VMEM((2, 8, NX, 64, PAD_D), BF16),
            pltpu.VMEM((2, 64, PICK), F32),
            pltpu.VMEM((2, 64, PAD_C), F32),
            pltpu.VMEM((2, 8, 16, 128), F32),
            pltpu.VMEM((2, 16, 128), BF16),
            pltpu.VMEM((2, NZ, NX, NY, 16, PAD_C), BF16),
            pltpu.VMEM((2, PAD_C, BLOCK), BF16),
            pltpu.VMEM((2, BLOCK, BLOCK), BF16),
            pltpu.VMEM((PICK, BLOCK), BF16),
            pltpu.SemaphoreType.DMA((N_SEMS,)),
            pltpu.SemaphoreType.DMA((N_SEMS,)),
            pltpu.SemaphoreType.DMA((24,)),
        ],
        compiler_params=pltpu.CompilerParams(
            collective_id=0, has_side_effects=True, vmem_limit_bytes=60 * 1024 * 1024),
        name="steps",
    )(owners, features.T, residual.T, coeffs.T, block_inverse, block_index)
    return new_coeffs.T, new_residual.T


def solution(mesh):
    both = ("rows", "cols")
    in_specs = (P(both, None), P(both, None), P(both, None), P(None, both, None),
                P(None, "cols"), P())
    out_specs = (P(both, None), P(both, None))
    return jax.shard_map(per_device, mesh=mesh, in_specs=in_specs, out_specs=out_specs,
                         check_vma=False)
```

```python
import functools
import math

import jax
import jax.numpy as jnp
from jax import lax
from jax.experimental import pallas as pl
from jax.experimental.pallas import tpu as pltpu
from jax.sharding import PartitionSpec as P

MESH = pl.DeviceIdType.MESH
NZ, NX, NY, NK = 8, 4, 4, 2
PICK = 256
BLOCK = 2048
PAD_D = 512
PAD_C = 256
PAD_R = 160
TILE = 256
F32 = jnp.float32
BF16 = jnp.bfloat16

STAGES = {
    "r_rsx": 4, "r_rsz": 8, "r_agz": 8, "r_agx": 4,
    "y_rsx": 8, "y_rsz": 8, "y_agz": 8, "y_ag2": 4, "y_ag3": 16, "y_core": 16,
    "p": 8, "u_agz": 8, "u_ag2": 4, "u_ag3": 16, "u_core": 16,
}
BASE = {}
_total = 0
for _name, _count in STAGES.items():
    BASE[_name] = _total
    _total += 2 * _count
BASE["b"] = _total
N_SEMS = _total + 8


def split3(value):
    hi = value.astype(BF16)
    rest = value - hi.astype(F32)
    mid = rest.astype(BF16)
    lo = (rest - mid.astype(F32)).astype(BF16)
    return hi.astype(F32), mid.astype(F32), lo.astype(F32)


def dot_t(a, b):
    return lax.dot_general(a, b, (((1,), (1,)), ((), ())), preferred_element_type=F32)


def with_norms(tail, squares, parts_at, ones_at, axis=1):
    lane = lax.broadcasted_iota(jnp.int32, tail.shape, axis)
    hi, mid, lo = split3(-0.5 * squares)
    out = jnp.where(lane < 56, tail, 0.0)
    out = jnp.where((lane >= ones_at) & (lane < ones_at + 3), 1.0, out)
    out = jnp.where(lane == parts_at, hi, out)
    out = jnp.where(lane == parts_at + 1, mid, out)
    return jnp.where(lane == parts_at + 2, lo, out)


def body(width, outs, owners, feat, res_in, co_in, binv_in, idxr, co_out, res_out,
         idxc, res, co, binv, xa, cho, rcho, rrx0, rrx1, rsel, rrz0, rrz1, rch, rbuf, rx0, rx1, sel, rz0, rz1, ych,
         ybuf, bg, pbuf, up, uch, ubuf, ut, kb, k21, ssem, rsem, lsem, osem):
    rrx, rrz, rx, rz = (rrx0, rrx1), (rrz0, rrz1), (rx0, rx1), (rz0, rz1)
    r = lax.axis_index("rows")
    c = lax.axis_index("cols")
    z, x = r // NX, r % NX
    y, k = c // NK, c % NK
    scale = 2.0 / width * math.log2(math.e)
    khalf = pl.ds(pl.multiple_of(k * 256, 256), 256)
    klane = pl.ds(pl.multiple_of(k * 128, 128), 128)
    tail_start = 384
    tail_used = width - tail_start

    def dev(zz, xx, yy, kk):
        return (zz * NX + xx, yy * NK + kk)

    desc = {}
    sent = []

    def when(need, action):
        if need is None:
            action()
        else:
            pl.when(need)(action)

    def send(name, s, i, src, dst, target, need=None):
        at = BASE[name] + (s * STAGES[name] + i if name in STAGES else i)
        copy = pltpu.make_async_remote_copy(
            src_ref=src, dst_ref=dst, send_sem=ssem.at[at], recv_sem=rsem.at[at],
            device_id=target, device_id_type=MESH)
        when(need, copy.start)
        desc[(name, s, i)] = copy
        sent.append((copy, need))

    def arrived(name, s, i, need=None):
        when(need, desc[(name, s, i)].wait_recv)

    def sends_done():
        for copy, need in sent:
            when(need, copy.wait_send)
        sent.clear()

    local_count = [0]

    def local(src, dst, need=None):
        copy = pltpu.make_async_copy(src, dst, lsem.at[local_count[0]])
        local_count[0] += 1
        when(need, copy.start)
        return copy

    peers = []
    for i in range(NX):
        for kk in range(NK):
            if (i, kk) != (0, 0):
                peers.append(dev(z, (x + i) % NX, y, (k + kk) % NK))
    for i in range(1, NZ):
        peers.append(dev((z + i) % NZ, x, y, k))
    for i in range(1, NY):
        for kk in range(NK):
            peers.append(dev(z, x, (y + i) % NY, (k + kk) % NK))
    barrier = pltpu.get_barrier_semaphore()
    for peer in peers:
        pl.semaphore_signal(barrier, inc=1, device_id=peer, device_id_type=MESH)

    copies = [local(res_in, res), local(feat, xa.at[0:width, :]), local(binv_in, binv),
              local(co_in, co)]
    rcho[...] = jnp.zeros_like(rcho)
    pbuf[...] = jnp.zeros_like(pbuf)
    diagonal = (lax.broadcasted_iota(jnp.int32, (PICK, PICK), 0)
                == lax.broadcasted_iota(jnp.int32, (PICK, PICK), 1))

    def chosen_at(s):
        index = jnp.broadcast_to(idxr[s:s + 1, :], (PICK, PICK))
        return jnp.sum(jnp.where(diagonal, index, 0).astype(F32), axis=1,
                       keepdims=True).astype(jnp.int32)

    def picks(s, start, size):
        position = lax.broadcasted_iota(jnp.int32, (PICK, size), 1) + start
        return jnp.where(idxc[s] == position, 1.0, 0.0)

    def choose_res(s):
        pick = picks(s, 0, BLOCK).astype(BF16)
        res_hi = res[...].astype(BF16)
        res_lo = (res[...] - res_hi.astype(F32)).astype(BF16)
        rcho[s, 0:outs, :] = dot_t(res_hi, pick) + dot_t(res_lo, pick)

    def choose_feat(s):
        pick = picks(s, 0, BLOCK).astype(BF16)
        rows = dot_t(pick, xa[0:width, :])
        squares = jnp.sum(rows * rows, axis=1, keepdims=True)
        cho[s, :, 0:width] = rows.astype(BF16)
        cho[s, :, tail_start:PAD_D] = with_norms(
            cho[s, :, tail_start:PAD_D].astype(F32), squares, tail_used + 3, tail_used).astype(BF16)

    for s in range(2):
        idxc[s] = chosen_at(s)
    copies[0].wait()
    choose_res(0)
    pl.semaphore_wait(barrier, len(peers))

    waits = {}

    def r_rsx(s):
        for i in range(1, NX):
            xx = (x + i) % NX
            send("r_rsx", s, i, rcho.at[s, pl.ds(pl.multiple_of(xx * 40, 8), 40), :],
                 rrx[s].at[x], dev(z, xx, y, k))
        waits[("r_rsx", s)] = local(
            rcho.at[s, pl.ds(pl.multiple_of(x * 40, 8), 40), :], rrx[s].at[x])

    def y_rsx(s):
        for i in range(NX):
            xx = (x + i) % NX
            for kk in range(NK):
                if (i, kk) == (0, 0):
                    continue
                k2 = (k + kk) % NK
                send("y_rsx", s, i * NK + kk,
                     cho.at[s, pl.ds(pl.multiple_of(xx * 64, 64), 64),
                            pl.ds(pl.multiple_of(k2 * 256, 256), 256)],
                     rx[s].at[x, k], dev(z, xx, y, k2))
        waits[("y_rsx", s)] = local(
            cho.at[s, pl.ds(pl.multiple_of(x * 64, 64), 64), khalf], rx[s].at[x, k])

    def r_rsz(s):
        for i in range(1, NX):
            arrived("r_rsx", s, i)
        waits[("r_rsx", s)].wait()
        rsel[s] = rrx[s][owners[s] % NX]
        for i in range(NZ):
            zz = (z + i) % NZ
            row = zz % 5
            src = rsel.at[s, pl.ds(pl.multiple_of(row * 8, 8), 8), :]
            if i == 0:
                waits[("r_rsz", s)] = local(src, rrz[s].at[z], zz < 5)
            else:
                send("r_rsz", s, i, src, rrz[s].at[z], dev(zz, x, y, k), zz < 5)

    def y_rsz(s):
        for i in range(NX):
            for kk in range(NK):
                if (i, kk) != (0, 0):
                    arrived("y_rsx", s, i * NK + kk)
        waits[("y_rsx", s)].wait()
        sel[s] = rx[s][owners[s] % NX]
        for i in range(NZ):
            zz = (z + i) % NZ
            src = sel.at[s, zz // 4, pl.ds(pl.multiple_of((zz % 4) * 16, 16), 16), :]
            if i == 0:
                waits[("y_rsz", s)] = local(src, rz[s].at[z])
            else:
                send("y_rsz", s, i, src, rz[s].at[z], dev(zz, x, y, k))

    def r_agz(s):
        place = rbuf.at[s, pl.ds(pl.multiple_of(x * 40 + (z % 5) * 8, 8), 8), :]
        for i in range(1, NZ):
            arrived("r_rsz", s, i, z < 5)

        @pl.when(z < 5)
        def _():
            waits[("r_rsz", s)].wait()
            rch[s] = rrz[s][owners[s] // NX]

        for i in range(1, NZ):
            send("r_agz", s, i, rch.at[s], place, dev((z + i) % NZ, x, y, k), z < 5)
        waits[("r_agz", s)] = local(rch.at[s], place, z < 5)

    def y_agz(s):
        for i in range(1, NZ):
            arrived("y_rsz", s, i)
        waits[("y_rsz", s)].wait()
        ych[s] = rz[s][owners[s] // NX]
        place = ybuf.at[s, 2 * y + z // 4, x,
                        pl.ds(pl.multiple_of((z % 4) * 16, 16), 16), khalf]
        for i in range(1, NZ):
            send("y_agz", s, i, ych.at[s], place, dev((z + i) % NZ, x, y, k))
        waits[("y_agz", s)] = local(ych.at[s], place)

    def r_agx(s):
        for i in range(1, NZ):
            arrived("r_agz", s, i, (z - i + NZ) % NZ < 5)
        when(z < 5, waits[("r_agz", s)].wait)
        part = rbuf.at[s, pl.ds(pl.multiple_of(x * 40, 8), 40), :]
        for i in range(1, NX):
            send("r_agx", s, i, part, part, dev(z, (x + i) % NX, y, k))

    g = (1 - k) * x + k * y
    q = (1 - k) * y + k * x

    def y_block(s, gg, qq):
        bx = (1 - k) * gg + k * qq
        by = k * gg + (1 - k) * qq
        return ybuf.at[s, pl.ds(2 * by, 2), bx, :, khalf]

    def u_block(s, gg, qq):
        bx = (1 - k) * gg + k * qq
        by = k * gg + (1 - k) * qq
        return ubuf.at[s, :, bx, by, :, klane]

    def to_second(i):
        return dev(z, (x + i * (1 - k)) % NX, (y + i * k) % NY, k)

    def to_third(i):
        return dev(z, (x + i * k) % NX, (y + i * (1 - k)) % NY, k)

    def to_core(kind, block, s, d, i):
        part = block(s, (g - d + NX) % NX, (q - i + NY) % NY)
        send(kind + "_core", s, d * 4 + i, part, part, dev(z, x, y, 1 - k))

    def ring_send(kind, block, s, d):
        part = block(s, (g - d + NX) % NX, q)
        for i in (1, 3):
            send(kind + "_ag3", s, d * 4 + i, part, part, to_third(i))
        to_core(kind, block, s, d, 0)

    def ring_pass(kind, block, s, d):
        for i, slot, half in ((1, 2, 0), (3, 0, 1)):
            arrived(kind + "_ag3", s, d * 4 + i)
            part = half_of(kind, block(s, (g - d + NX) % NX, (q - i + NY) % NY), half)
            send(kind + "_ag3", s, d * 4 + slot, part, part, to_third(i))
            to_core(kind, block, s, d, i)

    def half_of(kind, ref, half):
        if kind == "y":
            return ref.at[half:half + 1]
        return ref.at[half * 4:half * 4 + 4]

    def ag2_start(kind, block, s):
        for i in range(1, NZ):
            arrived(kind + "_agz", s, i)
        waits[(kind + "_agz", s)].wait()
        part = block(s, g, q)
        for i in range(1, NX):
            send(kind + "_ag2", s, i, part, part, to_second(i))
        ring_send(kind, block, s, 0)

    def ag3_start(kind, block, s):
        for d in range(1, NX):
            arrived(kind + "_ag2", s, d)
            ring_send(kind, block, s, d)

    def pass_start(kind, block, s):
        for d in range(NX):
            ring_pass(kind, block, s, d)

    def core_start(kind, block, s):
        for d in range(NX):
            arrived(kind + "_ag3", s, d * 4 + 2)
            arrived(kind + "_ag3", s, d * 4)
            to_core(kind, block, s, d, 2)

    def core_end(kind, s):
        for d in range(NX):
            for i in range(NY):
                arrived(kind + "_core", s, d * 4 + i)

    def inverse_times(s, values, dim):
        return lax.dot_general(bg[s], values, (((1,), (dim,)), ((), ())),
                               precision=lax.Precision.HIGHEST, preferred_element_type=F32)

    def partial_start(s):
        for i in range(NY * NK):
            cc = (c + i) % (NY * NK)
            src = pbuf.at[s, pl.ds(pl.multiple_of((cc // NK) * 16, 16), 16),
                          pl.ds(pl.multiple_of((cc % NK) * 128, 128), 128)]
            if i == 0:
                waits[("p", s)] = local(src, up.at[s, c])
            else:
                send("p", s, i, src, up.at[s, c], (r, cc))

    def u_agz(s):
        for i in range(1, NY * NK):
            arrived("p", s, i)
        waits[("p", s)].wait()
        uch[s] = jnp.sum(up[s], axis=0).astype(BF16)
        place = ubuf.at[s, z, x, y, :, klane]
        for i in range(1, NZ):
            send("u_agz", s, i, uch.at[s], place, dev((z + i) % NZ, x, y, k))
        waits[("u_agz", s)] = local(uch.at[s], place)

    def gen(s, first, last):
        @pl.loop(first, last)
        def _(t):
            at = pl.ds(pl.multiple_of(t * TILE, TILE), TILE)
            points = ybuf[s, t].reshape(TILE, PAD_D)
            for j in range(4):
                inner = jnp.dot(points, xa[:, j * 512:(j + 1) * 512], preferred_element_type=F32)
                kb[s, at, j * 512:(j + 1) * 512] = jnp.exp2(inner * scale).astype(BF16)

    def turn(s):
        ut[s] = jnp.transpose(ubuf[s].reshape(BLOCK, PAD_C))

    r_rsx(0)
    copies[2].wait()
    for i in range(NY * NK):
        cc = (c + i) % (NY * NK)
        src = binv.at[:, :, pl.ds(pl.multiple_of(cc * PICK, PICK), PICK)]
        dst = bg.at[:, pl.ds(pl.multiple_of(c * 8, 8), 8), :]
        if i == 0:
            waits["b"] = local(src, dst)
        else:
            send("b", 0, i, src, dst, (r, cc))
    copies[1].wait()
    choose_feat(0)
    r_rsz(0)
    y_rsx(0)
    choose_feat(1)
    y_rsx(1)
    choose_res(1)
    r_agz(0)
    y_rsz(0)

    @pl.loop(0, BLOCK // TILE)
    def _(t):
        at = pl.ds(pl.multiple_of(t * TILE, TILE), TILE)
        rows = xa[0:width, at].astype(F32)
        squares = jnp.sum(rows * rows, axis=0, keepdims=True)
        xa[tail_start:PAD_D, at] = with_norms(
            xa[tail_start:PAD_D, at].astype(F32), squares, tail_used, tail_used + 3, 0).astype(BF16)

    r_agx(0)
    y_rsz(1)
    r_rsx(1)
    y_agz(0)
    for i in range(1, NX):
        arrived("r_agx", 0, i)
    for i in range(1, NY * NK):
        arrived("b", 0, i)
    waits["b"].wait()
    pbuf[0, :, 0:PAD_R] = inverse_times(0, rbuf[0], 1)
    partial_start(0)
    ag2_start("y", y_block, 0)
    y_agz(1)
    r_rsz(1)
    u_agz(0)
    ag2_start("y", y_block, 1)
    ag3_start("y", y_block, 0)
    r_agz(1)
    ag2_start("u", u_block, 0)
    ag3_start("y", y_block, 1)
    pass_start("y", y_block, 0)
    ag3_start("u", u_block, 0)
    r_agx(1)
    pass_start("y", y_block, 1)
    pass_start("u", u_block, 0)
    core_start("y", y_block, 0)
    core_start("y", y_block, 1)
    core_start("u", u_block, 0)
    core_end("y", 0)
    core_end("y", 1)

    second = ybuf[1, c].reshape(PICK, PAD_D)
    tail = second[:, tail_start:PAD_D].astype(F32)
    lane = lax.broadcasted_iota(jnp.int32, tail.shape, 1)
    turned = pltpu.roll(tail, 125, 1)
    tail = jnp.where((lane >= tail_used) & (lane < tail_used + 3), turned, tail)
    tail = jnp.where((lane >= tail_used + 3) & (lane < tail_used + 6), 1.0, tail)
    second = jnp.concatenate([second[:, :tail_start], tail.astype(BF16)], axis=1)
    for j in range(4):
        inner = dot_t(second, ybuf[0, 2 * j:2 * j + 2].reshape(512, PAD_D))
        k21[:, j * 512:(j + 1) * 512] = jnp.exp2(inner * scale).astype(BF16)
    for i in range(1, NX):
        arrived("r_agx", 1, i)

    same = jnp.where(owners[0] == owners[1], 0.5, 0.0).astype(F32)
    twice = jnp.where(idxc[1] == idxr[0:1, :], same, 0.0).astype(BF16)
    pbuf[1, :, 0:PAD_R] = inverse_times(1, rbuf[1], 1)
    core_end("u", 0)
    moved = jnp.dot(k21[...], ubuf[0].reshape(BLOCK, PAD_C), preferred_element_type=F32)
    moved += jnp.dot(twice, ubuf[0, c].reshape(PICK, PAD_C), preferred_element_type=F32)
    pbuf[1] = pbuf[1] - inverse_times(1, moved, 0)
    partial_start(1)
    turn(0)
    mine = pl.ds(pl.multiple_of(c * PICK, PICK), PICK)

    def product(s, t):
        at = pl.ds(pl.multiple_of(t * 512, 512), 512)
        change = jnp.dot(ut[s, 0:PAD_R, :], kb[s, :, at], preferred_element_type=F32)
        own = jnp.where(owners[s] == r, 1.0, 0.0).astype(F32)
        put = (picks(s, t * 512, 512) * own).astype(BF16)
        added = jnp.dot(ut[s, 0:PAD_R, mine], put, preferred_element_type=F32)
        res[:, at] = res[:, at] - (change + 0.5 * added)[:outs, :]
        co[:, at] = co[:, at] + added[:outs, :]

    def out_copies(t):
        at = pl.ds(pl.multiple_of(t * 512, 512), 512)
        return (pltpu.make_async_copy(res.at[:, at], res_out.at[:, at], osem.at[0, t]),
                pltpu.make_async_copy(co.at[:, at], co_out.at[:, at], osem.at[1, t]))

    gen(0, 0, 4)
    u_agz(1)
    gen(0, 4, 8)
    copies[3].wait()
    ag2_start("u", u_block, 1)

    @pl.loop(0, 4)
    def _(t):
        product(0, t)

    sends_done()
    ag3_start("u", u_block, 1)
    gen(1, 0, 4)
    pass_start("u", u_block, 1)
    gen(1, 4, 8)
    core_start("u", u_block, 1)
    sends_done()
    core_end("u", 1)
    turn(1)

    @pl.loop(0, 4)
    def _(t):
        product(1, t)

        @pl.when(t > 0)
        def _():
            for copy in out_copies(t - 1):
                copy.start()

    for copy in out_copies(3):
        copy.start()
    for t in range(4):
        for copy in out_copies(t):
            copy.wait()


def per_device(features, residual, coeffs, block_inverse, block_index, owners):
    frames, width = features.shape
    outs = residual.shape[1]
    vmem = pl.BlockSpec(memory_space=pltpu.VMEM)
    new_coeffs, new_residual = pl.pallas_call(
        functools.partial(body, width, outs),
        out_shape=(jax.ShapeDtypeStruct((outs, frames), F32),
                   jax.ShapeDtypeStruct((outs, frames), F32)),
        in_specs=[pl.BlockSpec(memory_space=pltpu.SMEM)] + [pl.BlockSpec(memory_space=pl.ANY)] * 4 + [vmem],
        out_specs=(pl.BlockSpec(memory_space=pl.ANY),) * 2,
        scratch_shapes=[
            pltpu.VMEM((2, PICK, 1), jnp.int32),
            pltpu.VMEM((outs, BLOCK), F32),
            pltpu.VMEM((outs, BLOCK), F32),
            pltpu.VMEM((2, 8, BLOCK), F32),
            pltpu.VMEM((PAD_D, BLOCK), BF16),
            pltpu.VMEM((2, PICK, PAD_D), BF16),
            pltpu.VMEM((2, PAD_R, PICK), F32),
            pltpu.VMEM((NX, 40, PICK), F32),
            pltpu.VMEM((NX, 40, PICK), F32),
            pltpu.VMEM((2, 40, PICK), F32),
            pltpu.VMEM((NZ, 8, PICK), F32),
            pltpu.VMEM((NZ, 8, PICK), F32),
            pltpu.VMEM((2, 8, PICK), F32),
            pltpu.VMEM((2, PAD_R, PICK), F32),
            pltpu.VMEM((NX, NK, 64, 256), BF16),
            pltpu.VMEM((NX, NK, 64, 256), BF16),
            pltpu.VMEM((2, NK, 64, 256), BF16),
            pltpu.VMEM((NZ, 16, 256), BF16),
            pltpu.VMEM((NZ, 16, 256), BF16),
            pltpu.VMEM((2, 16, 256), BF16),
            pltpu.VMEM((2, 8, NX, 64, PAD_D), BF16),
            pltpu.VMEM((2, 64, PICK), F32),
            pltpu.VMEM((2, 64, PAD_C), F32),
            pltpu.VMEM((2, 8, 16, 128), F32),
            pltpu.VMEM((2, 16, 128), BF16),
            pltpu.VMEM((2, NZ, NX, NY, 16, PAD_C), BF16),
            pltpu.VMEM((2, PAD_C, BLOCK), BF16),
            pltpu.VMEM((2, BLOCK, BLOCK), BF16),
            pltpu.VMEM((PICK, BLOCK), BF16),
            pltpu.SemaphoreType.DMA((N_SEMS,)),
            pltpu.SemaphoreType.DMA((N_SEMS,)),
            pltpu.SemaphoreType.DMA((24,)),
            pltpu.SemaphoreType.DMA((2, 4)),
        ],
        compiler_params=pltpu.CompilerParams(
            collective_id=0, has_side_effects=True, vmem_limit_bytes=50 * 1024 * 1024),
        name="steps",
    )(*[pltpu.with_memory_space_constraint(v, pltpu.HBM) for v in
          (owners, features.T, residual.T, coeffs.T, block_inverse, block_index)])
    return new_coeffs.T, new_residual.T


def solution(mesh):
    both = ("rows", "cols")
    in_specs = (P(both, None), P(both, None), P(both, None), P(None, both, None),
                P(None, "cols"), P())
    out_specs = (P(both, None), P(both, None))
    return jax.shard_map(per_device, mesh=mesh, in_specs=in_specs, out_specs=out_specs,
                         check_vma=False)
```

```python
import functools
import math

import jax
import jax.numpy as jnp
from jax import lax
from jax.experimental import pallas as pl
from jax.experimental.pallas import tpu as pltpu
from jax.sharding import PartitionSpec as P

MESH = pl.DeviceIdType.MESH
NZ, NX, NY, NK = 8, 4, 4, 2
PICK = 256
BLOCK = 2048
PAD_D = 512
PAD_C = 256
PAD_R = 160
TILE = 256
F32 = jnp.float32
BF16 = jnp.bfloat16

STAGES = {
    "r_rsx": 4, "r_rsz": 8, "r_agz": 8, "r_agx": 4,
    "y_rsx": 8, "y_rsz": 8, "y_agz": 8, "y_ag2": 4, "y_ag3": 16, "y_core": 16,
    "p": 8, "u_agz": 8, "u_ag2": 4, "u_ag3": 16, "u_core": 16,
}
BASE = {}
_total = 0
for _name, _count in STAGES.items():
    BASE[_name] = _total
    _total += 2 * _count
BASE["b"] = _total
N_SEMS = _total + 8


def split3(value):
    hi = value.astype(BF16)
    rest = value - hi.astype(F32)
    mid = rest.astype(BF16)
    lo = (rest - mid.astype(F32)).astype(BF16)
    return hi.astype(F32), mid.astype(F32), lo.astype(F32)


def dot_t(a, b):
    return lax.dot_general(a, b, (((1,), (1,)), ((), ())), preferred_element_type=F32)


def with_norms(tail, squares, parts_at, ones_at, axis=1):
    lane = lax.broadcasted_iota(jnp.int32, tail.shape, axis)
    hi, mid, lo = split3(-0.5 * squares)
    out = jnp.where(lane < 56, tail, 0.0)
    out = jnp.where((lane >= ones_at) & (lane < ones_at + 3), 1.0, out)
    out = jnp.where(lane == parts_at, hi, out)
    out = jnp.where(lane == parts_at + 1, mid, out)
    return jnp.where(lane == parts_at + 2, lo, out)


def body(width, outs, owners, feat, res_in, co_in, binv_in, idxr, co_out, res_out,
         idxc, res, co, binv, xa, cho, rcho, rrx0, rrx1, rsel, rrz0, rrz1, rch, rbuf, rx0, rx1, sel, rz0, rz1, ych,
         ybuf, bg, pbuf, up, uch, ubuf, ut, kb, k21, ssem, rsem, lsem, osem):
    rrx, rrz, rx, rz = (rrx0, rrx1), (rrz0, rrz1), (rx0, rx1), (rz0, rz1)
    r = lax.axis_index("rows")
    c = lax.axis_index("cols")
    z, x = r // NX, r % NX
    y, k = c // NK, c % NK
    scale = 2.0 / width * math.log2(math.e)
    khalf = pl.ds(pl.multiple_of(k * 256, 256), 256)
    klane = pl.ds(pl.multiple_of(k * 128, 128), 128)
    tail_start = 384
    tail_used = width - tail_start

    def dev(zz, xx, yy, kk):
        return (zz * NX + xx, yy * NK + kk)

    desc = {}
    sent = []

    def when(need, action):
        if need is None:
            action()
        else:
            pl.when(need)(action)

    def send(name, s, i, src, dst, target, need=None):
        at = BASE[name] + (s * STAGES[name] + i if name in STAGES else i)
        copy = pltpu.make_async_remote_copy(
            src_ref=src, dst_ref=dst, send_sem=ssem.at[at], recv_sem=rsem.at[at],
            device_id=target, device_id_type=MESH)
        when(need, copy.start)
        desc[(name, s, i)] = copy
        sent.append((copy, need))

    def arrived(name, s, i, need=None):
        when(need, desc[(name, s, i)].wait_recv)

    def sends_done():
        for copy, need in sent:
            when(need, copy.wait_send)
        sent.clear()

    local_count = [0]

    def local(src, dst, need=None):
        copy = pltpu.make_async_copy(src, dst, lsem.at[local_count[0]])
        local_count[0] += 1
        when(need, copy.start)
        return copy

    peers = []
    for i in range(NX):
        for kk in range(NK):
            if (i, kk) != (0, 0):
                peers.append(dev(z, (x + i) % NX, y, (k + kk) % NK))
    for i in range(1, NZ):
        peers.append(dev((z + i) % NZ, x, y, k))
    for i in range(1, NY):
        for kk in range(NK):
            peers.append(dev(z, x, (y + i) % NY, (k + kk) % NK))
    barrier = pltpu.get_barrier_semaphore()
    for peer in peers:
        pl.semaphore_signal(barrier, inc=1, device_id=peer, device_id_type=MESH)

    copies = [local(res_in, res), local(feat, xa.at[0:width, :]), local(binv_in, binv),
              local(co_in, co)]
    rcho[...] = jnp.zeros_like(rcho)
    pbuf[...] = jnp.zeros_like(pbuf)
    diagonal = (lax.broadcasted_iota(jnp.int32, (PICK, PICK), 0)
                == lax.broadcasted_iota(jnp.int32, (PICK, PICK), 1))

    def chosen_at(s):
        index = jnp.broadcast_to(idxr[s:s + 1, :], (PICK, PICK))
        return jnp.sum(jnp.where(diagonal, index, 0).astype(F32), axis=1,
                       keepdims=True).astype(jnp.int32)

    def picks(s, start, size):
        position = lax.broadcasted_iota(jnp.int32, (PICK, size), 1) + start
        return jnp.where(idxc[s] == position, 1.0, 0.0)

    def choose_res(s):
        pick = picks(s, 0, BLOCK).astype(BF16)
        res_hi = res[...].astype(BF16)
        res_lo = (res[...] - res_hi.astype(F32)).astype(BF16)
        rcho[s, 0:outs, :] = dot_t(res_hi, pick) + dot_t(res_lo, pick)

    def choose_feat(s):
        pick = picks(s, 0, BLOCK).astype(BF16)
        rows = dot_t(pick, xa[0:width, :])
        squares = jnp.sum(rows * rows, axis=1, keepdims=True)
        cho[s, :, 0:width] = rows.astype(BF16)
        cho[s, :, tail_start:PAD_D] = with_norms(
            cho[s, :, tail_start:PAD_D].astype(F32), squares, tail_used + 3, tail_used).astype(BF16)

    for s in range(2):
        idxc[s] = chosen_at(s)
    copies[0].wait()
    choose_res(0)
    pl.semaphore_wait(barrier, len(peers))

    waits = {}

    def r_rsx(s):
        for i in range(1, NX):
            xx = (x + i) % NX
            send("r_rsx", s, i, rcho.at[s, pl.ds(pl.multiple_of(xx * 40, 8), 40), :],
                 rrx[s].at[x], dev(z, xx, y, k))
        waits[("r_rsx", s)] = local(
            rcho.at[s, pl.ds(pl.multiple_of(x * 40, 8), 40), :], rrx[s].at[x])

    def y_rsx(s):
        for i in range(NX):
            xx = (x + i) % NX
            for kk in range(NK):
                if (i, kk) == (0, 0):
                    continue
                k2 = (k + kk) % NK
                send("y_rsx", s, i * NK + kk,
                     cho.at[s, pl.ds(pl.multiple_of(xx * 64, 64), 64),
                            pl.ds(pl.multiple_of(k2 * 256, 256), 256)],
                     rx[s].at[x, k], dev(z, xx, y, k2))
        waits[("y_rsx", s)] = local(
            cho.at[s, pl.ds(pl.multiple_of(x * 64, 64), 64), khalf], rx[s].at[x, k])

    def r_rsz(s):
        for i in range(1, NX):
            arrived("r_rsx", s, i)
        waits[("r_rsx", s)].wait()
        rsel[s] = rrx[s][owners[s] % NX]
        for i in range(NZ):
            zz = (z + i) % NZ
            row = zz % 5
            src = rsel.at[s, pl.ds(pl.multiple_of(row * 8, 8), 8), :]
            if i == 0:
                waits[("r_rsz", s)] = local(src, rrz[s].at[z], zz < 5)
            else:
                send("r_rsz", s, i, src, rrz[s].at[z], dev(zz, x, y, k), zz < 5)

    def y_rsz(s):
        for i in range(NX):
            for kk in range(NK):
                if (i, kk) != (0, 0):
                    arrived("y_rsx", s, i * NK + kk)
        waits[("y_rsx", s)].wait()
        sel[s] = rx[s][owners[s] % NX]
        for i in range(NZ):
            zz = (z + i) % NZ
            src = sel.at[s, zz // 4, pl.ds(pl.multiple_of((zz % 4) * 16, 16), 16), :]
            if i == 0:
                waits[("y_rsz", s)] = local(src, rz[s].at[z])
            else:
                send("y_rsz", s, i, src, rz[s].at[z], dev(zz, x, y, k))

    def r_agz(s):
        place = rbuf.at[s, pl.ds(pl.multiple_of(x * 40 + (z % 5) * 8, 8), 8), :]
        for i in range(1, NZ):
            arrived("r_rsz", s, i, z < 5)

        @pl.when(z < 5)
        def _():
            waits[("r_rsz", s)].wait()
            rch[s] = rrz[s][owners[s] // NX]

        for i in range(1, NZ):
            send("r_agz", s, i, rch.at[s], place, dev((z + i) % NZ, x, y, k), z < 5)
        waits[("r_agz", s)] = local(rch.at[s], place, z < 5)

    def y_agz(s):
        for i in range(1, NZ):
            arrived("y_rsz", s, i)
        waits[("y_rsz", s)].wait()
        ych[s] = rz[s][owners[s] // NX]
        place = ybuf.at[s, 2 * y + z // 4, x,
                        pl.ds(pl.multiple_of((z % 4) * 16, 16), 16), khalf]
        for i in range(1, NZ):
            send("y_agz", s, i, ych.at[s], place, dev((z + i) % NZ, x, y, k))
        waits[("y_agz", s)] = local(ych.at[s], place)

    def r_agx(s):
        for i in range(1, NZ):
            arrived("r_agz", s, i, (z - i + NZ) % NZ < 5)
        when(z < 5, waits[("r_agz", s)].wait)
        part = rbuf.at[s, pl.ds(pl.multiple_of(x * 40, 8), 40), :]
        for i in range(1, NX):
            send("r_agx", s, i, part, part, dev(z, (x + i) % NX, y, k))

    g = (1 - k) * x + k * y
    q = (1 - k) * y + k * x

    def y_block(s, gg, qq):
        bx = (1 - k) * gg + k * qq
        by = k * gg + (1 - k) * qq
        return ybuf.at[s, pl.ds(2 * by, 2), bx, :, khalf]

    def u_block(s, gg, qq):
        bx = (1 - k) * gg + k * qq
        by = k * gg + (1 - k) * qq
        return ubuf.at[s, :, bx, by, :, klane]

    def to_second(i):
        return dev(z, (x + i * (1 - k)) % NX, (y + i * k) % NY, k)

    def to_third(i):
        return dev(z, (x + i * k) % NX, (y + i * (1 - k)) % NY, k)

    def to_core(kind, block, s, d, i):
        part = block(s, (g - d + NX) % NX, (q - i + NY) % NY)
        send(kind + "_core", s, d * 4 + i, part, part, dev(z, x, y, 1 - k))

    def ring_send(kind, block, s, d):
        part = block(s, (g - d + NX) % NX, q)
        for i in (1, 3):
            send(kind + "_ag3", s, d * 4 + i, part, part, to_third(i))
        to_core(kind, block, s, d, 0)

    def ring_pass(kind, block, s, d):
        for i, slot, half in ((1, 2, 0), (3, 0, 1)):
            arrived(kind + "_ag3", s, d * 4 + i)
            part = half_of(kind, block(s, (g - d + NX) % NX, (q - i + NY) % NY), half)
            send(kind + "_ag3", s, d * 4 + slot, part, part, to_third(i))
            to_core(kind, block, s, d, i)

    def half_of(kind, ref, half):
        if kind == "y":
            return ref.at[half:half + 1]
        return ref.at[half * 4:half * 4 + 4]

    def ag2_start(kind, block, s):
        for i in range(1, NZ):
            arrived(kind + "_agz", s, i)
        waits[(kind + "_agz", s)].wait()
        part = block(s, g, q)
        for i in range(1, NX):
            send(kind + "_ag2", s, i, part, part, to_second(i))
        ring_send(kind, block, s, 0)

    def ag3_start(kind, block, s):
        for d in range(1, NX):
            arrived(kind + "_ag2", s, d)
            ring_send(kind, block, s, d)

    def pass_start(kind, block, s):
        for d in range(NX):
            ring_pass(kind, block, s, d)

    def core_start(kind, block, s):
        for d in range(NX):
            arrived(kind + "_ag3", s, d * 4 + 2)
            arrived(kind + "_ag3", s, d * 4)
            to_core(kind, block, s, d, 2)

    def core_end(kind, s):
        for d in range(NX):
            for i in range(NY):
                arrived(kind + "_core", s, d * 4 + i)

    def inverse_times(s, values, dim):
        return lax.dot_general(bg[s], values, (((1,), (dim,)), ((), ())),
                               precision=lax.Precision.HIGHEST, preferred_element_type=F32)

    def partial_start(s):
        for i in range(NY * NK):
            cc = (c + i) % (NY * NK)
            src = pbuf.at[s, pl.ds(pl.multiple_of((cc // NK) * 16, 16), 16),
                          pl.ds(pl.multiple_of((cc % NK) * 128, 128), 128)]
            if i == 0:
                waits[("p", s)] = local(src, up.at[s, c])
            else:
                send("p", s, i, src, up.at[s, c], (r, cc))

    def u_agz(s):
        for i in range(1, NY * NK):
            arrived("p", s, i)
        waits[("p", s)].wait()
        uch[s] = jnp.sum(up[s], axis=0).astype(BF16)
        place = ubuf.at[s, z, x, y, :, klane]
        for i in range(1, NZ):
            send("u_agz", s, i, uch.at[s], place, dev((z + i) % NZ, x, y, k))
        waits[("u_agz", s)] = local(uch.at[s], place)

    def gen(s, first, last):
        @pl.loop(first, last)
        def _(t):
            at = pl.ds(pl.multiple_of(t * TILE, TILE), TILE)
            points = ybuf[s, t].reshape(TILE, PAD_D)
            for j in range(4):
                inner = jnp.dot(points, xa[:, j * 512:(j + 1) * 512], preferred_element_type=F32)
                kb[s, at, j * 512:(j + 1) * 512] = jnp.exp2(inner * scale).astype(BF16)

    def turn(s):
        ut[s] = jnp.transpose(ubuf[s].reshape(BLOCK, PAD_C))

    r_rsx(0)
    copies[2].wait()
    for i in range(NY * NK):
        cc = (c + i) % (NY * NK)
        src = binv.at[:, :, pl.ds(pl.multiple_of(cc * PICK, PICK), PICK)]
        dst = bg.at[:, pl.ds(pl.multiple_of(c * 8, 8), 8), :]
        if i == 0:
            waits["b"] = local(src, dst)
        else:
            send("b", 0, i, src, dst, (r, cc))
    copies[1].wait()
    choose_feat(0)
    y_rsx(0)
    choose_feat(1)
    y_rsx(1)
    r_rsz(0)
    choose_res(1)
    y_rsz(0)
    r_agz(0)

    @pl.loop(0, BLOCK // TILE)
    def _(t):
        at = pl.ds(pl.multiple_of(t * TILE, TILE), TILE)
        rows = xa[0:width, at].astype(F32)
        squares = jnp.sum(rows * rows, axis=0, keepdims=True)
        xa[tail_start:PAD_D, at] = with_norms(
            xa[tail_start:PAD_D, at].astype(F32), squares, tail_used, tail_used + 3, 0).astype(BF16)

    y_rsz(1)
    y_agz(0)
    r_agx(0)
    r_rsx(1)
    y_agz(1)
    ag2_start("y", y_block, 0)
    for i in range(1, NX):
        arrived("r_agx", 0, i)
    for i in range(1, NY * NK):
        arrived("b", 0, i)
    waits["b"].wait()
    pbuf[0, :, 0:PAD_R] = inverse_times(0, rbuf[0], 1)
    partial_start(0)
    r_rsz(1)
    ag2_start("y", y_block, 1)
    u_agz(0)
    ag3_start("y", y_block, 0)
    r_agz(1)
    ag3_start("y", y_block, 1)
    pass_start("y", y_block, 0)
    ag2_start("u", u_block, 0)
    core_start("y", y_block, 0)
    pass_start("y", y_block, 1)
    ag3_start("u", u_block, 0)
    r_agx(1)
    core_start("y", y_block, 1)
    pass_start("u", u_block, 0)
    core_start("u", u_block, 0)
    core_end("y", 0)
    core_end("y", 1)

    second = ybuf[1, c].reshape(PICK, PAD_D)
    tail = second[:, tail_start:PAD_D].astype(F32)
    lane = lax.broadcasted_iota(jnp.int32, tail.shape, 1)
    turned = pltpu.roll(tail, 125, 1)
    tail = jnp.where((lane >= tail_used) & (lane < tail_used + 3), turned, tail)
    tail = jnp.where((lane >= tail_used + 3) & (lane < tail_used + 6), 1.0, tail)
    second = jnp.concatenate([second[:, :tail_start], tail.astype(BF16)], axis=1)
    for j in range(4):
        inner = dot_t(second, ybuf[0, 2 * j:2 * j + 2].reshape(512, PAD_D))
        k21[:, j * 512:(j + 1) * 512] = jnp.exp2(inner * scale).astype(BF16)
    for i in range(1, NX):
        arrived("r_agx", 1, i)

    same = jnp.where(owners[0] == owners[1], 0.5, 0.0).astype(F32)
    twice = jnp.where(idxc[1] == idxr[0:1, :], same, 0.0).astype(BF16)
    pbuf[1, :, 0:PAD_R] = inverse_times(1, rbuf[1], 1)
    core_end("u", 0)
    moved = jnp.dot(k21[...], ubuf[0].reshape(BLOCK, PAD_C), preferred_element_type=F32)
    moved += jnp.dot(twice, ubuf[0, c].reshape(PICK, PAD_C), preferred_element_type=F32)
    pbuf[1] = pbuf[1] - inverse_times(1, moved, 0)
    partial_start(1)
    turn(0)
    mine = pl.ds(pl.multiple_of(c * PICK, PICK), PICK)

    def product(s, t, low, high):
        at = pl.ds(pl.multiple_of(t * 512, 512), 512)
        change = jnp.dot(ut[s, low:high, :], kb[s, :, at], preferred_element_type=F32)
        own = jnp.where(owners[s] == r, 1.0, 0.0).astype(F32)
        put = (picks(s, t * 512, 512) * own).astype(BF16)
        added = jnp.dot(ut[s, low:high, mine], put, preferred_element_type=F32)
        top = min(high, outs)
        res[low:top, at] = res[low:top, at] - (change + 0.5 * added)[:top - low, :]
        co[low:top, at] = co[low:top, at] + added[:top - low, :]

    def turn_half(h):
        ut[1, h * 128:(h + 1) * 128, :] = jnp.transpose(
            ubuf[1, :, :, :, :, h * 128:(h + 1) * 128].reshape(BLOCK, 128))

    def out_copies(t):
        at = pl.ds(pl.multiple_of(t * 512, 512), 512)
        return (pltpu.make_async_copy(res.at[:, at], res_out.at[:, at], osem.at[0, t]),
                pltpu.make_async_copy(co.at[:, at], co_out.at[:, at], osem.at[1, t]))

    gen(0, 0, 4)
    u_agz(1)
    gen(0, 4, 8)
    copies[3].wait()
    ag2_start("u", u_block, 1)

    @pl.loop(0, 4)
    def _(t):
        product(0, t, 0, PAD_R)

    sends_done()
    ag3_start("u", u_block, 1)
    gen(1, 0, 4)
    pass_start("u", u_block, 1)
    gen(1, 4, 8)
    sends_done()
    core_start("u", u_block, 1)
    for h, (low, high) in enumerate(((0, 128), (128, PAD_R))):
        @pl.when(k == h)
        def _():
            turn_half(h)

            @pl.loop(0, 4)
            def _(t):
                product(1, t, low, high)

    core_end("u", 1)
    for h, (low, high) in enumerate(((0, 128), (128, PAD_R))):
        @pl.when(k == 1 - h)
        def _():
            turn_half(h)

            @pl.loop(0, 4)
            def _(t):
                product(1, t, low, high)

                @pl.when(t > 0)
                def _():
                    for copy in out_copies(t - 1):
                        copy.start()

    for copy in out_copies(3):
        copy.start()
    sends_done()
    for t in range(4):
        for copy in out_copies(t):
            copy.wait()


def per_device(features, residual, coeffs, block_inverse, block_index, owners):
    frames, width = features.shape
    outs = residual.shape[1]
    vmem = pl.BlockSpec(memory_space=pltpu.VMEM)
    new_coeffs, new_residual = pl.pallas_call(
        functools.partial(body, width, outs),
        out_shape=(jax.ShapeDtypeStruct((outs, frames), F32),
                   jax.ShapeDtypeStruct((outs, frames), F32)),
        in_specs=[pl.BlockSpec(memory_space=pltpu.SMEM)] + [pl.BlockSpec(memory_space=pl.ANY)] * 4 + [vmem],
        out_specs=(pl.BlockSpec(memory_space=pl.ANY),) * 2,
        scratch_shapes=[
            pltpu.VMEM((2, PICK, 1), jnp.int32),
            pltpu.VMEM((outs, BLOCK), F32),
            pltpu.VMEM((outs, BLOCK), F32),
            pltpu.VMEM((2, 8, BLOCK), F32),
            pltpu.VMEM((PAD_D, BLOCK), BF16),
            pltpu.VMEM((2, PICK, PAD_D), BF16),
            pltpu.VMEM((2, PAD_R, PICK), F32),
            pltpu.VMEM((NX, 40, PICK), F32),
            pltpu.VMEM((NX, 40, PICK), F32),
            pltpu.VMEM((2, 40, PICK), F32),
            pltpu.VMEM((NZ, 8, PICK), F32),
            pltpu.VMEM((NZ, 8, PICK), F32),
            pltpu.VMEM((2, 8, PICK), F32),
            pltpu.VMEM((2, PAD_R, PICK), F32),
            pltpu.VMEM((NX, NK, 64, 256), BF16),
            pltpu.VMEM((NX, NK, 64, 256), BF16),
            pltpu.VMEM((2, NK, 64, 256), BF16),
            pltpu.VMEM((NZ, 16, 256), BF16),
            pltpu.VMEM((NZ, 16, 256), BF16),
            pltpu.VMEM((2, 16, 256), BF16),
            pltpu.VMEM((2, 8, NX, 64, PAD_D), BF16),
            pltpu.VMEM((2, 64, PICK), F32),
            pltpu.VMEM((2, 64, PAD_C), F32),
            pltpu.VMEM((2, 8, 16, 128), F32),
            pltpu.VMEM((2, 16, 128), BF16),
            pltpu.VMEM((2, NZ, NX, NY, 16, PAD_C), BF16),
            pltpu.VMEM((2, PAD_C, BLOCK), BF16),
            pltpu.VMEM((2, BLOCK, BLOCK), BF16),
            pltpu.VMEM((PICK, BLOCK), BF16),
            pltpu.SemaphoreType.DMA((N_SEMS,)),
            pltpu.SemaphoreType.DMA((N_SEMS,)),
            pltpu.SemaphoreType.DMA((24,)),
            pltpu.SemaphoreType.DMA((2, 4)),
        ],
        compiler_params=pltpu.CompilerParams(
            collective_id=0, has_side_effects=True, vmem_limit_bytes=50 * 1024 * 1024),
        name="steps",
    )(*[pltpu.with_memory_space_constraint(v, pltpu.HBM) for v in
          (owners, features.T, residual.T, coeffs.T, block_inverse, block_index)])
    return new_coeffs.T, new_residual.T


def solution(mesh):
    both = ("rows", "cols")
    in_specs = (P(both, None), P(both, None), P(both, None), P(None, both, None),
                P(None, "cols"), P())
    out_specs = (P(both, None), P(both, None))
    return jax.shard_map(per_device, mesh=mesh, in_specs=in_specs, out_specs=out_specs,
                         check_vma=False)
```

```python
import functools
import math

import jax
import jax.numpy as jnp
from jax import lax
from jax.experimental import pallas as pl
from jax.experimental.pallas import tpu as pltpu
from jax.sharding import PartitionSpec as P

MESH = pl.DeviceIdType.MESH
NZ, NX, NY, NK = 8, 4, 4, 2
PICK = 256
BLOCK = 2048
PAD_D = 512
PAD_C = 256
PAD_R = 160
TILE = 256
F32 = jnp.float32
BF16 = jnp.bfloat16

STAGES = {
    "r_rsx": 4, "r_rsz": 8, "r_agz": 8, "r_agx": 4,
    "y_rsx": 8, "y_rsz": 8, "y_agz": 8, "y_ag2": 4, "y_ag3": 16, "y_core": 16,
    "p": 8, "u_agz": 8, "u_ag2": 4, "u_ag3": 16, "u_core": 16,
}
BASE = {}
_total = 0
for _name, _count in STAGES.items():
    BASE[_name] = _total
    _total += 2 * _count
BASE["b"] = _total
N_SEMS = _total + 8


def split3(value):
    hi = value.astype(BF16)
    rest = value - hi.astype(F32)
    mid = rest.astype(BF16)
    lo = (rest - mid.astype(F32)).astype(BF16)
    return hi.astype(F32), mid.astype(F32), lo.astype(F32)


def dot_t(a, b):
    return lax.dot_general(a, b, (((1,), (1,)), ((), ())), preferred_element_type=F32)


def with_norms(tail, squares, parts_at, ones_at, axis=1):
    lane = lax.broadcasted_iota(jnp.int32, tail.shape, axis)
    hi, mid, lo = split3(-0.5 * squares)
    out = jnp.where(lane < 56, tail, 0.0)
    out = jnp.where((lane >= ones_at) & (lane < ones_at + 3), 1.0, out)
    out = jnp.where(lane == parts_at, hi, out)
    out = jnp.where(lane == parts_at + 1, mid, out)
    return jnp.where(lane == parts_at + 2, lo, out)


def body(width, outs, owners, feat, res_in, co_in, binv_in, idxr, co_out, res_out,
         idxc, res, co, binv, xa, cho, rcho, rrx0, rrx1, rsel, rrz0, rrz1, rch, rbuf, rx0, rx1, sel, rz0, rz1, ych,
         ybuf, bg, pbuf, up, uch, ubuf, ut, kb, k21, ssem, rsem, lsem, osem):
    rrx, rrz, rx, rz = (rrx0, rrx1), (rrz0, rrz1), (rx0, rx1), (rz0, rz1)
    r = lax.axis_index("rows")
    c = lax.axis_index("cols")
    z, x = r // NX, r % NX
    y, k = c // NK, c % NK
    scale = 2.0 / width * math.log2(math.e)
    khalf = pl.ds(pl.multiple_of(k * 256, 256), 256)
    klane = pl.ds(pl.multiple_of(k * 128, 128), 128)
    tail_start = 384
    tail_used = width - tail_start

    def dev(zz, xx, yy, kk):
        return (zz * NX + xx, yy * NK + kk)

    desc = {}
    sent = []

    def when(need, action):
        if need is None:
            action()
        else:
            pl.when(need)(action)

    def send(name, s, i, src, dst, target, need=None):
        at = BASE[name] + (s * STAGES[name] + i if name in STAGES else i)
        copy = pltpu.make_async_remote_copy(
            src_ref=src, dst_ref=dst, send_sem=ssem.at[at], recv_sem=rsem.at[at],
            device_id=target, device_id_type=MESH)
        when(need, copy.start)
        desc[(name, s, i)] = copy
        sent.append((copy, need))

    def arrived(name, s, i, need=None):
        when(need, desc[(name, s, i)].wait_recv)

    def sends_done():
        for copy, need in sent:
            when(need, copy.wait_send)
        sent.clear()

    local_count = [0]

    def local(src, dst, need=None):
        copy = pltpu.make_async_copy(src, dst, lsem.at[local_count[0]])
        local_count[0] += 1
        when(need, copy.start)
        return copy

    peers = []
    for i in range(NX):
        for kk in range(NK):
            if (i, kk) != (0, 0):
                peers.append(dev(z, (x + i) % NX, y, (k + kk) % NK))
    for i in range(1, NZ):
        peers.append(dev((z + i) % NZ, x, y, k))
    for i in range(1, NY):
        for kk in range(NK):
            peers.append(dev(z, x, (y + i) % NY, (k + kk) % NK))
    barrier = pltpu.get_barrier_semaphore()
    for peer in peers:
        pl.semaphore_signal(barrier, inc=1, device_id=peer, device_id_type=MESH)

    copies = [local(res_in, res), local(feat, xa.at[0:width, :]), local(binv_in, binv),
              local(co_in, co)]
    rcho[...] = jnp.zeros_like(rcho)
    pbuf[...] = jnp.zeros_like(pbuf)
    diagonal = (lax.broadcasted_iota(jnp.int32, (PICK, PICK), 0)
                == lax.broadcasted_iota(jnp.int32, (PICK, PICK), 1))

    def chosen_at(s):
        index = jnp.broadcast_to(idxr[s:s + 1, :], (PICK, PICK))
        return jnp.sum(jnp.where(diagonal, index, 0).astype(F32), axis=1,
                       keepdims=True).astype(jnp.int32)

    def picks(s, start, size):
        position = lax.broadcasted_iota(jnp.int32, (PICK, size), 1) + start
        return jnp.where(idxc[s] == position, 1.0, 0.0)

    def choose_res(s):
        pick = picks(s, 0, BLOCK).astype(BF16)
        res_hi = res[...].astype(BF16)
        res_lo = (res[...] - res_hi.astype(F32)).astype(BF16)
        rcho[s, 0:outs, :] = dot_t(res_hi, pick) + dot_t(res_lo, pick)

    def choose_feat(s):
        pick = picks(s, 0, BLOCK).astype(BF16)
        rows = dot_t(pick, xa[0:width, :])
        squares = jnp.sum(rows * rows, axis=1, keepdims=True)
        cho[s, :, 0:width] = rows.astype(BF16)
        cho[s, :, tail_start:PAD_D] = with_norms(
            cho[s, :, tail_start:PAD_D].astype(F32), squares, tail_used + 3, tail_used).astype(BF16)

    for s in range(2):
        idxc[s] = chosen_at(s)
    copies[0].wait()
    choose_res(0)
    pl.semaphore_wait(barrier, len(peers))

    waits = {}

    def r_rsx(s):
        for i in range(1, NX):
            xx = (x + i) % NX
            send("r_rsx", s, i, rcho.at[s, pl.ds(pl.multiple_of(xx * 40, 8), 40), :],
                 rrx[s].at[x], dev(z, xx, y, k))
        waits[("r_rsx", s)] = local(
            rcho.at[s, pl.ds(pl.multiple_of(x * 40, 8), 40), :], rrx[s].at[x])

    def y_rsx(s):
        for i in range(NX):
            xx = (x + i) % NX
            for kk in range(NK):
                if (i, kk) == (0, 0):
                    continue
                k2 = (k + kk) % NK
                send("y_rsx", s, i * NK + kk,
                     cho.at[s, pl.ds(pl.multiple_of(xx * 64, 64), 64),
                            pl.ds(pl.multiple_of(k2 * 256, 256), 256)],
                     rx[s].at[x, k], dev(z, xx, y, k2))
        waits[("y_rsx", s)] = local(
            cho.at[s, pl.ds(pl.multiple_of(x * 64, 64), 64), khalf], rx[s].at[x, k])

    def r_rsz(s):
        for i in range(1, NX):
            arrived("r_rsx", s, i)
        waits[("r_rsx", s)].wait()
        rsel[s] = rrx[s][owners[s] % NX]
        for i in range(NZ):
            zz = (z + i) % NZ
            row = zz % 5
            src = rsel.at[s, pl.ds(pl.multiple_of(row * 8, 8), 8), :]
            if i == 0:
                waits[("r_rsz", s)] = local(src, rrz[s].at[z], zz < 5)
            else:
                send("r_rsz", s, i, src, rrz[s].at[z], dev(zz, x, y, k), zz < 5)

    def y_rsz(s):
        for i in range(NX):
            for kk in range(NK):
                if (i, kk) != (0, 0):
                    arrived("y_rsx", s, i * NK + kk)
        waits[("y_rsx", s)].wait()
        sel[s] = rx[s][owners[s] % NX]
        for i in range(NZ):
            zz = (z + i) % NZ
            src = sel.at[s, zz // 4, pl.ds(pl.multiple_of((zz % 4) * 16, 16), 16), :]
            if i == 0:
                waits[("y_rsz", s)] = local(src, rz[s].at[z])
            else:
                send("y_rsz", s, i, src, rz[s].at[z], dev(zz, x, y, k))

    def r_agz(s):
        place = rbuf.at[s, pl.ds(pl.multiple_of(x * 40 + (z % 5) * 8, 8), 8), :]
        for i in range(1, NZ):
            arrived("r_rsz", s, i, z < 5)

        @pl.when(z < 5)
        def _():
            waits[("r_rsz", s)].wait()
            rch[s] = rrz[s][owners[s] // NX]

        for i in range(1, NZ):
            send("r_agz", s, i, rch.at[s], place, dev((z + i) % NZ, x, y, k), z < 5)
        waits[("r_agz", s)] = local(rch.at[s], place, z < 5)

    def y_agz(s):
        for i in range(1, NZ):
            arrived("y_rsz", s, i)
        waits[("y_rsz", s)].wait()
        ych[s] = rz[s][owners[s] // NX]
        place = ybuf.at[s, 2 * y + z // 4, x,
                        pl.ds(pl.multiple_of((z % 4) * 16, 16), 16), khalf]
        for i in range(1, NZ):
            send("y_agz", s, i, ych.at[s], place, dev((z + i) % NZ, x, y, k))
        waits[("y_agz", s)] = local(ych.at[s], place)

    def r_agx(s):
        for i in range(1, NZ):
            arrived("r_agz", s, i, (z - i + NZ) % NZ < 5)
        when(z < 5, waits[("r_agz", s)].wait)
        part = rbuf.at[s, pl.ds(pl.multiple_of(x * 40, 8), 40), :]
        for i in range(1, NX):
            send("r_agx", s, i, part, part, dev(z, (x + i) % NX, y, k))

    g = (1 - k) * x + k * y
    q = (1 - k) * y + k * x

    def y_block(s, gg, qq):
        bx = (1 - k) * gg + k * qq
        by = k * gg + (1 - k) * qq
        return ybuf.at[s, pl.ds(2 * by, 2), bx, :, khalf]

    def u_block(s, gg, qq):
        bx = (1 - k) * gg + k * qq
        by = k * gg + (1 - k) * qq
        return ubuf.at[s, :, bx, by, :, klane]

    def to_second(i):
        return dev(z, (x + i * (1 - k)) % NX, (y + i * k) % NY, k)

    def to_third(i):
        return dev(z, (x + i * k) % NX, (y + i * (1 - k)) % NY, k)

    def to_core(kind, block, s, d, i):
        part = block(s, (g - d + NX) % NX, (q - i + NY) % NY)
        send(kind + "_core", s, d * 4 + i, part, part, dev(z, x, y, 1 - k))

    def ring_send(kind, block, s, d):
        part = block(s, (g - d + NX) % NX, q)
        for i in (1, 3):
            send(kind + "_ag3", s, d * 4 + i, part, part, to_third(i))
        to_core(kind, block, s, d, 0)

    def ring_pass(kind, block, s, d):
        for i, slot, half in ((1, 2, 0), (3, 0, 1)):
            arrived(kind + "_ag3", s, d * 4 + i)
            part = half_of(kind, block(s, (g - d + NX) % NX, (q - i + NY) % NY), half)
            send(kind + "_ag3", s, d * 4 + slot, part, part, to_third(i))
            to_core(kind, block, s, d, i)

    def half_of(kind, ref, half):
        if kind == "y":
            return ref.at[half:half + 1]
        return ref.at[half * 4:half * 4 + 4]

    def ag2_start(kind, block, s):
        for i in range(1, NZ):
            arrived(kind + "_agz", s, i)
        waits[(kind + "_agz", s)].wait()
        part = block(s, g, q)
        for i in range(1, NX):
            send(kind + "_ag2", s, i, part, part, to_second(i))
        ring_send(kind, block, s, 0)

    def ag3_start(kind, block, s):
        for d in range(1, NX):
            arrived(kind + "_ag2", s, d)
            ring_send(kind, block, s, d)

    def pass_start(kind, block, s):
        for d in range(NX):
            ring_pass(kind, block, s, d)

    def core_start(kind, block, s):
        for d in range(NX):
            arrived(kind + "_ag3", s, d * 4 + 2)
            arrived(kind + "_ag3", s, d * 4)
            to_core(kind, block, s, d, 2)

    def core_end(kind, s):
        for d in range(NX):
            for i in range(NY):
                arrived(kind + "_core", s, d * 4 + i)

    def inverse_times(s, values, dim):
        return lax.dot_general(bg[s], values, (((1,), (dim,)), ((), ())),
                               precision=lax.Precision.HIGHEST, preferred_element_type=F32)

    def partial_start(s):
        for i in range(NY * NK):
            cc = (c + i) % (NY * NK)
            src = pbuf.at[s, pl.ds(pl.multiple_of((cc // NK) * 16, 16), 16),
                          pl.ds(pl.multiple_of((cc % NK) * 128, 128), 128)]
            if i == 0:
                waits[("p", s)] = local(src, up.at[s, c])
            else:
                send("p", s, i, src, up.at[s, c], (r, cc))

    def u_agz(s):
        for i in range(1, NY * NK):
            arrived("p", s, i)
        waits[("p", s)].wait()
        uch[s] = jnp.sum(up[s], axis=0).astype(BF16)
        place = ubuf.at[s, z, x, y, :, klane]
        for i in range(1, NZ):
            send("u_agz", s, i, uch.at[s], place, dev((z + i) % NZ, x, y, k))
        waits[("u_agz", s)] = local(uch.at[s], place)

    def gen(s, first, last):
        @pl.loop(first, last)
        def _(t):
            at = pl.ds(pl.multiple_of(t * TILE, TILE), TILE)
            points = ybuf[s, t].reshape(TILE, PAD_D)
            for j in range(4):
                inner = jnp.dot(points, xa[:, j * 512:(j + 1) * 512], preferred_element_type=F32)
                kb[s, at, j * 512:(j + 1) * 512] = jnp.exp2(inner * scale).astype(BF16)

    def turn(s):
        ut[s] = jnp.transpose(ubuf[s].reshape(BLOCK, PAD_C))

    r_rsx(0)
    copies[2].wait()
    for i in range(NY * NK):
        cc = (c + i) % (NY * NK)
        src = binv.at[:, :, pl.ds(pl.multiple_of(cc * PICK, PICK), PICK)]
        dst = bg.at[:, pl.ds(pl.multiple_of(c * 8, 8), 8), :]
        if i == 0:
            waits["b"] = local(src, dst)
        else:
            send("b", 0, i, src, dst, (r, cc))
    copies[1].wait()
    choose_feat(0)
    y_rsx(0)
    choose_feat(1)
    y_rsx(1)
    r_rsz(0)
    choose_res(1)
    y_rsz(0)
    r_agz(0)

    @pl.loop(0, BLOCK // TILE)
    def _(t):
        at = pl.ds(pl.multiple_of(t * TILE, TILE), TILE)
        rows = xa[0:width, at].astype(F32)
        squares = jnp.sum(rows * rows, axis=0, keepdims=True)
        xa[tail_start:PAD_D, at] = with_norms(
            xa[tail_start:PAD_D, at].astype(F32), squares, tail_used, tail_used + 3, 0).astype(BF16)

    y_rsz(1)
    y_agz(0)
    r_agx(0)
    y_agz(1)
    ag2_start("y", y_block, 0)
    r_rsx(1)
    for i in range(1, NX):
        arrived("r_agx", 0, i)
    for i in range(1, NY * NK):
        arrived("b", 0, i)
    waits["b"].wait()
    pbuf[0, :, 0:PAD_R] = inverse_times(0, rbuf[0], 1)
    partial_start(0)
    ag2_start("y", y_block, 1)
    u_agz(0)
    r_rsz(1)
    ag3_start("y", y_block, 0)
    ag3_start("y", y_block, 1)
    pass_start("y", y_block, 0)
    ag2_start("u", u_block, 0)
    r_agz(1)
    core_start("y", y_block, 0)
    pass_start("y", y_block, 1)
    ag3_start("u", u_block, 0)
    r_agx(1)
    core_start("y", y_block, 1)
    pass_start("u", u_block, 0)
    core_start("u", u_block, 0)
    for i in range(1, NX):
        arrived("r_agx", 1, i)
    pbuf[1, :, 0:PAD_R] = inverse_times(1, rbuf[1], 1)
    core_end("y", 0)
    core_end("y", 1)

    second = ybuf[1, c].reshape(PICK, PAD_D)
    tail = second[:, tail_start:PAD_D].astype(F32)
    lane = lax.broadcasted_iota(jnp.int32, tail.shape, 1)
    turned = pltpu.roll(tail, 125, 1)
    tail = jnp.where((lane >= tail_used) & (lane < tail_used + 3), turned, tail)
    tail = jnp.where((lane >= tail_used + 3) & (lane < tail_used + 6), 1.0, tail)
    second = jnp.concatenate([second[:, :tail_start], tail.astype(BF16)], axis=1)
    for j in range(4):
        inner = dot_t(second, ybuf[0, 2 * j:2 * j + 2].reshape(512, PAD_D))
        k21[:, j * 512:(j + 1) * 512] = jnp.exp2(inner * scale).astype(BF16)
    same = jnp.where(owners[0] == owners[1], 0.5, 0.0).astype(F32)
    twice = jnp.where(idxc[1] == idxr[0:1, :], same, 0.0).astype(BF16)
    core_end("u", 0)
    moved = jnp.dot(k21[...], ubuf[0].reshape(BLOCK, PAD_C), preferred_element_type=F32)
    moved += jnp.dot(twice, ubuf[0, c].reshape(PICK, PAD_C), preferred_element_type=F32)
    pbuf[1] = pbuf[1] - inverse_times(1, moved, 0)
    partial_start(1)
    turn(0)
    mine = pl.ds(pl.multiple_of(c * PICK, PICK), PICK)

    def product(s, t, low, high):
        at = pl.ds(pl.multiple_of(t * 512, 512), 512)
        change = jnp.dot(ut[s, low:high, :], kb[s, :, at], preferred_element_type=F32)
        own = jnp.where(owners[s] == r, 1.0, 0.0).astype(F32)
        put = (picks(s, t * 512, 512) * own).astype(BF16)
        added = jnp.dot(ut[s, low:high, mine], put, preferred_element_type=F32)
        top = min(high, outs)
        res[low:top, at] = res[low:top, at] - (change + 0.5 * added)[:top - low, :]
        co[low:top, at] = co[low:top, at] + added[:top - low, :]

    def turn_half(h):
        ut[1, h * 128:(h + 1) * 128, :] = jnp.transpose(
            ubuf[1, :, :, :, :, h * 128:(h + 1) * 128].reshape(BLOCK, 128))

    def out_copies(t):
        at = pl.ds(pl.multiple_of(t * 512, 512), 512)
        return (pltpu.make_async_copy(res.at[:, at], res_out.at[:, at], osem.at[0, t]),
                pltpu.make_async_copy(co.at[:, at], co_out.at[:, at], osem.at[1, t]))

    gen(0, 0, 4)
    u_agz(1)
    gen(0, 4, 8)
    sends_done()
    copies[3].wait()
    ag2_start("u", u_block, 1)

    @pl.loop(0, 4)
    def _(t):
        product(0, t, 0, PAD_R)

    ag3_start("u", u_block, 1)
    gen(1, 0, 4)
    pass_start("u", u_block, 1)
    gen(1, 4, 8)
    sends_done()
    core_start("u", u_block, 1)
    for h, (low, high) in enumerate(((0, 128), (128, PAD_R))):
        @pl.when(k == h)
        def _():
            turn_half(h)

            @pl.loop(0, 4)
            def _(t):
                product(1, t, low, high)

    core_end("u", 1)
    for h, (low, high) in enumerate(((0, 128), (128, PAD_R))):
        @pl.when(k == 1 - h)
        def _():
            turn_half(h)

            @pl.loop(0, 4)
            def _(t):
                product(1, t, low, high)

                @pl.when(t > 0)
                def _():
                    for copy in out_copies(t - 1):
                        copy.start()

    for copy in out_copies(3):
        copy.start()
    sends_done()
    for t in range(4):
        for copy in out_copies(t):
            copy.wait()


def per_device(features, residual, coeffs, block_inverse, block_index, owners):
    frames, width = features.shape
    outs = residual.shape[1]
    vmem = pl.BlockSpec(memory_space=pltpu.VMEM)
    new_coeffs, new_residual = pl.pallas_call(
        functools.partial(body, width, outs),
        out_shape=(jax.ShapeDtypeStruct((outs, frames), F32),
                   jax.ShapeDtypeStruct((outs, frames), F32)),
        in_specs=[pl.BlockSpec(memory_space=pltpu.SMEM)] + [pl.BlockSpec(memory_space=pl.ANY)] * 4 + [vmem],
        out_specs=(pl.BlockSpec(memory_space=pl.ANY),) * 2,
        scratch_shapes=[
            pltpu.VMEM((2, PICK, 1), jnp.int32),
            pltpu.VMEM((outs, BLOCK), F32),
            pltpu.VMEM((outs, BLOCK), F32),
            pltpu.VMEM((2, 8, BLOCK), F32),
            pltpu.VMEM((PAD_D, BLOCK), BF16),
            pltpu.VMEM((2, PICK, PAD_D), BF16),
            pltpu.VMEM((2, PAD_R, PICK), F32),
            pltpu.VMEM((NX, 40, PICK), F32),
            pltpu.VMEM((NX, 40, PICK), F32),
            pltpu.VMEM((2, 40, PICK), F32),
            pltpu.VMEM((NZ, 8, PICK), F32),
            pltpu.VMEM((NZ, 8, PICK), F32),
            pltpu.VMEM((2, 8, PICK), F32),
            pltpu.VMEM((2, PAD_R, PICK), F32),
            pltpu.VMEM((NX, NK, 64, 256), BF16),
            pltpu.VMEM((NX, NK, 64, 256), BF16),
            pltpu.VMEM((2, NK, 64, 256), BF16),
            pltpu.VMEM((NZ, 16, 256), BF16),
            pltpu.VMEM((NZ, 16, 256), BF16),
            pltpu.VMEM((2, 16, 256), BF16),
            pltpu.VMEM((2, 8, NX, 64, PAD_D), BF16),
            pltpu.VMEM((2, 64, PICK), F32),
            pltpu.VMEM((2, 64, PAD_C), F32),
            pltpu.VMEM((2, 8, 16, 128), F32),
            pltpu.VMEM((2, 16, 128), BF16),
            pltpu.VMEM((2, NZ, NX, NY, 16, PAD_C), BF16),
            pltpu.VMEM((2, PAD_C, BLOCK), BF16),
            pltpu.VMEM((2, BLOCK, BLOCK), BF16),
            pltpu.VMEM((PICK, BLOCK), BF16),
            pltpu.SemaphoreType.DMA((N_SEMS,)),
            pltpu.SemaphoreType.DMA((N_SEMS,)),
            pltpu.SemaphoreType.DMA((24,)),
            pltpu.SemaphoreType.DMA((2, 4)),
        ],
        compiler_params=pltpu.CompilerParams(
            collective_id=0, has_side_effects=True, vmem_limit_bytes=50 * 1024 * 1024),
        name="steps",
    )(*[pltpu.with_memory_space_constraint(v, pltpu.HBM) for v in
          (owners, features.T, residual.T, coeffs.T, block_inverse, block_index)])
    return new_coeffs.T, new_residual.T


def solution(mesh):
    both = ("rows", "cols")
    in_specs = (P(both, None), P(both, None), P(both, None), P(None, both, None),
                P(None, "cols"), P())
    out_specs = (P(both, None), P(both, None))
    return jax.shard_map(per_device, mesh=mesh, in_specs=in_specs, out_specs=out_specs,
                         check_vma=False)
```

```python
import functools
import math

import jax
import jax.numpy as jnp
from jax import lax
from jax.experimental import pallas as pl
from jax.experimental.pallas import tpu as pltpu
from jax.sharding import PartitionSpec as P

MESH = pl.DeviceIdType.MESH
NZ, NX, NY, NK = 8, 4, 4, 2
PICK = 256
BLOCK = 2048
PAD_D = 512
PAD_C = 256
PAD_R = 160
TILE = 256
F32 = jnp.float32
BF16 = jnp.bfloat16

STAGES = {
    "r_rsx": 4, "r_rsz": 8, "r_agz": 8, "r_agx": 4,
    "y_rsx": 8, "y_rsz": 8, "y_agz": 8, "y_ag2": 4, "y_ag3": 16, "y_core": 16,
    "p": 8, "u_agz": 8, "u_ag2": 4, "u_ag3": 16, "u_core": 16,
}
BASE = {}
_total = 0
for _name, _count in STAGES.items():
    BASE[_name] = _total
    _total += 2 * _count
BASE["b"] = _total
N_SEMS = _total + 8


def split3(value):
    hi = value.astype(BF16)
    rest = value - hi.astype(F32)
    mid = rest.astype(BF16)
    lo = (rest - mid.astype(F32)).astype(BF16)
    return hi.astype(F32), mid.astype(F32), lo.astype(F32)


def dot_t(a, b):
    return lax.dot_general(a, b, (((1,), (1,)), ((), ())), preferred_element_type=F32)


def with_norms(tail, squares, parts_at, ones_at, axis=1):
    lane = lax.broadcasted_iota(jnp.int32, tail.shape, axis)
    hi, mid, lo = split3(-0.5 * squares)
    out = jnp.where(lane < 56, tail, 0.0)
    out = jnp.where((lane >= ones_at) & (lane < ones_at + 3), 1.0, out)
    out = jnp.where(lane == parts_at, hi, out)
    out = jnp.where(lane == parts_at + 1, mid, out)
    return jnp.where(lane == parts_at + 2, lo, out)


def body(width, outs, owners, feat, res_in, co_in, binv_in, idxr, co_out, res_out,
         idxc, res, co, binv, xa, cho, rcho, rrx0, rrx1, rsel, rrz0, rrz1, rch, rbuf, rx0, rx1, sel, rz0, rz1, ych,
         ybuf, bg, pbuf, up, uch, ubuf, ut, kb, k21, ssem, rsem, lsem, osem):
    rrx, rrz, rx, rz = (rrx0, rrx1), (rrz0, rrz1), (rx0, rx1), (rz0, rz1)
    r = lax.axis_index("rows")
    c = lax.axis_index("cols")
    z, x = r // NX, r % NX
    y, k = c // NK, c % NK
    scale = 2.0 / width * math.log2(math.e)
    khalf = pl.ds(pl.multiple_of(k * 256, 256), 256)
    klane = pl.ds(pl.multiple_of(k * 128, 128), 128)
    tail_start = 384
    tail_used = width - tail_start

    def dev(zz, xx, yy, kk):
        return (zz * NX + xx, yy * NK + kk)

    desc = {}
    sent = []

    def when(need, action):
        if need is None:
            action()
        else:
            pl.when(need)(action)

    def send(name, s, i, src, dst, target, need=None):
        at = BASE[name] + (s * STAGES[name] + i if name in STAGES else i)
        copy = pltpu.make_async_remote_copy(
            src_ref=src, dst_ref=dst, send_sem=ssem.at[at], recv_sem=rsem.at[at],
            device_id=target, device_id_type=MESH)
        when(need, copy.start)
        desc[(name, s, i)] = copy
        sent.append((copy, need))

    def arrived(name, s, i, need=None):
        when(need, desc[(name, s, i)].wait_recv)

    def sends_done():
        for copy, need in sent:
            when(need, copy.wait_send)
        sent.clear()

    local_count = [0]

    def local(src, dst, need=None):
        copy = pltpu.make_async_copy(src, dst, lsem.at[local_count[0]])
        local_count[0] += 1
        when(need, copy.start)
        return copy

    peers = []
    for i in range(NX):
        for kk in range(NK):
            if (i, kk) != (0, 0):
                peers.append(dev(z, (x + i) % NX, y, (k + kk) % NK))
    for i in range(1, NZ):
        peers.append(dev((z + i) % NZ, x, y, k))
    for i in range(1, NY):
        for kk in range(NK):
            peers.append(dev(z, x, (y + i) % NY, (k + kk) % NK))
    barrier = pltpu.get_barrier_semaphore()
    for peer in peers:
        pl.semaphore_signal(barrier, inc=1, device_id=peer, device_id_type=MESH)

    copies = [local(res_in, res), local(feat, xa.at[0:width, :]), local(binv_in, binv),
              local(co_in, co)]
    rcho[...] = jnp.zeros_like(rcho)
    pbuf[...] = jnp.zeros_like(pbuf)
    diagonal = (lax.broadcasted_iota(jnp.int32, (PICK, PICK), 0)
                == lax.broadcasted_iota(jnp.int32, (PICK, PICK), 1))

    def chosen_at(s):
        index = jnp.broadcast_to(idxr[s:s + 1, :], (PICK, PICK))
        return jnp.sum(jnp.where(diagonal, index, 0).astype(F32), axis=1,
                       keepdims=True).astype(jnp.int32)

    def picks(s, start, size):
        position = lax.broadcasted_iota(jnp.int32, (PICK, size), 1) + start
        return jnp.where(idxc[s] == position, 1.0, 0.0)

    def choose_res(s):
        pick = picks(s, 0, BLOCK).astype(BF16)
        res_hi = res[...].astype(BF16)
        res_lo = (res[...] - res_hi.astype(F32)).astype(BF16)
        rcho[s, 0:outs, :] = dot_t(res_hi, pick) + dot_t(res_lo, pick)

    def choose_feat(s):
        pick = picks(s, 0, BLOCK).astype(BF16)
        rows = dot_t(pick, xa[0:width, :])
        squares = jnp.sum(rows * rows, axis=1, keepdims=True)
        cho[s, :, 0:width] = rows.astype(BF16)
        cho[s, :, tail_start:PAD_D] = with_norms(
            cho[s, :, tail_start:PAD_D].astype(F32), squares, tail_used + 3, tail_used).astype(BF16)

    for s in range(2):
        idxc[s] = chosen_at(s)
    copies[0].wait()
    choose_res(0)
    pl.semaphore_wait(barrier, len(peers))

    waits = {}

    def r_rsx(s):
        for i in range(1, NX):
            xx = (x + i) % NX
            send("r_rsx", s, i, rcho.at[s, pl.ds(pl.multiple_of(xx * 40, 8), 40), :],
                 rrx[s].at[x], dev(z, xx, y, k))
        waits[("r_rsx", s)] = local(
            rcho.at[s, pl.ds(pl.multiple_of(x * 40, 8), 40), :], rrx[s].at[x])

    def y_rsx(s):
        for i in range(NX):
            xx = (x + i) % NX
            for kk in range(NK):
                if (i, kk) == (0, 0):
                    continue
                k2 = (k + kk) % NK
                send("y_rsx", s, i * NK + kk,
                     cho.at[s, pl.ds(pl.multiple_of(xx * 64, 64), 64),
                            pl.ds(pl.multiple_of(k2 * 256, 256), 256)],
                     rx[s].at[x, k], dev(z, xx, y, k2))
        waits[("y_rsx", s)] = local(
            cho.at[s, pl.ds(pl.multiple_of(x * 64, 64), 64), khalf], rx[s].at[x, k])

    def r_rsz(s):
        for i in range(1, NX):
            arrived("r_rsx", s, i)
        waits[("r_rsx", s)].wait()
        rsel[s] = rrx[s][owners[s] % NX]
        for i in range(NZ):
            zz = (z + i) % NZ
            row = zz % 5
            src = rsel.at[s, pl.ds(pl.multiple_of(row * 8, 8), 8), :]
            if i == 0:
                waits[("r_rsz", s)] = local(src, rrz[s].at[z], zz < 5)
            else:
                send("r_rsz", s, i, src, rrz[s].at[z], dev(zz, x, y, k), zz < 5)

    def y_rsz(s):
        for i in range(NX):
            for kk in range(NK):
                if (i, kk) != (0, 0):
                    arrived("y_rsx", s, i * NK + kk)
        waits[("y_rsx", s)].wait()
        sel[s] = rx[s][owners[s] % NX]
        for i in range(NZ):
            zz = (z + i) % NZ
            src = sel.at[s, zz // 4, pl.ds(pl.multiple_of((zz % 4) * 16, 16), 16), :]
            if i == 0:
                waits[("y_rsz", s)] = local(src, rz[s].at[z])
            else:
                send("y_rsz", s, i, src, rz[s].at[z], dev(zz, x, y, k))

    def r_agz(s):
        place = rbuf.at[s, pl.ds(pl.multiple_of(x * 40 + (z % 5) * 8, 8), 8), :]
        for i in range(1, NZ):
            arrived("r_rsz", s, i, z < 5)

        @pl.when(z < 5)
        def _():
            waits[("r_rsz", s)].wait()
            rch[s] = rrz[s][owners[s] // NX]

        for i in range(1, NZ):
            send("r_agz", s, i, rch.at[s], place, dev((z + i) % NZ, x, y, k), z < 5)
        waits[("r_agz", s)] = local(rch.at[s], place, z < 5)

    def y_agz(s):
        for i in range(1, NZ):
            arrived("y_rsz", s, i)
        waits[("y_rsz", s)].wait()
        ych[s] = rz[s][owners[s] // NX]
        place = ybuf.at[s, 2 * y + z // 4, x,
                        pl.ds(pl.multiple_of((z % 4) * 16, 16), 16), khalf]
        for i in range(1, NZ):
            send("y_agz", s, i, ych.at[s], place, dev((z + i) % NZ, x, y, k))
        waits[("y_agz", s)] = local(ych.at[s], place)

    def r_agx(s):
        for i in range(1, NZ):
            arrived("r_agz", s, i, (z - i + NZ) % NZ < 5)
        when(z < 5, waits[("r_agz", s)].wait)
        part = rbuf.at[s, pl.ds(pl.multiple_of(x * 40, 8), 40), :]
        for i in (1, 3):
            send("r_agx", s, i, part, part, dev(z, (x + i) % NX, y, k))

    def r_agx_pass(s):
        for i, slot, first, rows in ((1, 2, 0, 24), (3, 0, 24, 16)):
            arrived("r_agx", s, i)
            start = ((x - i + NX) % NX) * 40 + first
            part = rbuf.at[s, pl.ds(pl.multiple_of(start, 8), rows), :]
            send("r_agx", s, slot, part, part, dev(z, (x + i) % NX, y, k))

    g = (1 - k) * x + k * y
    q = (1 - k) * y + k * x

    def y_block(s, gg, qq):
        bx = (1 - k) * gg + k * qq
        by = k * gg + (1 - k) * qq
        return ybuf.at[s, pl.ds(2 * by, 2), bx, :, khalf]

    def u_block(s, gg, qq):
        bx = (1 - k) * gg + k * qq
        by = k * gg + (1 - k) * qq
        return ubuf.at[s, :, bx, by, :, klane]

    def to_second(i):
        return dev(z, (x + i * (1 - k)) % NX, (y + i * k) % NY, k)

    def to_third(i):
        return dev(z, (x + i * k) % NX, (y + i * (1 - k)) % NY, k)

    def to_core(kind, block, s, d, i):
        part = block(s, (g - d + NX) % NX, (q - i + NY) % NY)
        send(kind + "_core", s, d * 4 + i, part, part, dev(z, x, y, 1 - k))

    def ring_send(kind, block, s, d):
        part = block(s, (g - d + NX) % NX, q)
        for i in (1, 3):
            send(kind + "_ag3", s, d * 4 + i, part, part, to_third(i))
        to_core(kind, block, s, d, 0)

    def ring_pass(kind, block, s, d):
        for i, slot, half in ((1, 2, 0), (3, 0, 1)):
            arrived(kind + "_ag3", s, d * 4 + i)
            part = half_of(kind, block(s, (g - d + NX) % NX, (q - i + NY) % NY), half)
            send(kind + "_ag3", s, d * 4 + slot, part, part, to_third(i))
            to_core(kind, block, s, d, i)

    def half_of(kind, ref, half):
        if kind == "y":
            return ref.at[half:half + 1]
        return ref.at[half * 4:half * 4 + 4]

    def ag2_start(kind, block, s):
        for i in range(1, NZ):
            arrived(kind + "_agz", s, i)
        waits[(kind + "_agz", s)].wait()
        part = block(s, g, q)
        for i in range(1, NX):
            send(kind + "_ag2", s, i, part, part, to_second(i))
        ring_send(kind, block, s, 0)

    def ag3_start(kind, block, s):
        for d in range(1, NX):
            arrived(kind + "_ag2", s, d)
            ring_send(kind, block, s, d)

    def pass_start(kind, block, s):
        for d in range(NX):
            ring_pass(kind, block, s, d)

    def core_start(kind, block, s):
        for d in range(NX):
            arrived(kind + "_ag3", s, d * 4 + 2)
            arrived(kind + "_ag3", s, d * 4)
            to_core(kind, block, s, d, 2)

    def core_end(kind, s):
        for d in range(NX):
            for i in range(NY):
                arrived(kind + "_core", s, d * 4 + i)

    def inverse_times(s, values, dim):
        return lax.dot_general(bg[s], values, (((1,), (dim,)), ((), ())),
                               precision=lax.Precision.HIGHEST, preferred_element_type=F32)

    def partial_start(s):
        for i in range(NY * NK):
            cc = (c + i) % (NY * NK)
            src = pbuf.at[s, pl.ds(pl.multiple_of((cc // NK) * 16, 16), 16),
                          pl.ds(pl.multiple_of((cc % NK) * 128, 128), 128)]
            if i == 0:
                waits[("p", s)] = local(src, up.at[s, c])
            else:
                send("p", s, i, src, up.at[s, c], (r, cc))

    def u_agz(s):
        for i in range(1, NY * NK):
            arrived("p", s, i)
        waits[("p", s)].wait()
        uch[s] = jnp.sum(up[s], axis=0).astype(BF16)
        place = ubuf.at[s, z, x, y, :, klane]
        for i in range(1, NZ):
            send("u_agz", s, i, uch.at[s], place, dev((z + i) % NZ, x, y, k))
        waits[("u_agz", s)] = local(uch.at[s], place)

    def gen(s, first, last):
        @pl.loop(first, last)
        def _(t):
            at = pl.ds(pl.multiple_of(t * TILE, TILE), TILE)
            points = ybuf[s, t].reshape(TILE, PAD_D)
            for j in range(4):
                inner = jnp.dot(points, xa[:, j * 512:(j + 1) * 512], preferred_element_type=F32)
                kb[s, at, j * 512:(j + 1) * 512] = jnp.exp2(inner * scale).astype(BF16)

    def turn(s):
        ut[s] = jnp.transpose(ubuf[s].reshape(BLOCK, PAD_C))

    r_rsx(0)
    copies[2].wait()
    for i in range(NY * NK):
        cc = (c + i) % (NY * NK)
        src = binv.at[:, :, pl.ds(pl.multiple_of(cc * PICK, PICK), PICK)]
        dst = bg.at[:, pl.ds(pl.multiple_of(c * 8, 8), 8), :]
        if i == 0:
            waits["b"] = local(src, dst)
        else:
            send("b", 0, i, src, dst, (r, cc))
    copies[1].wait()
    choose_feat(0)
    y_rsx(0)
    choose_feat(1)
    y_rsx(1)
    r_rsz(0)
    choose_res(1)
    y_rsz(0)
    r_agz(0)

    @pl.loop(0, BLOCK // TILE)
    def _(t):
        at = pl.ds(pl.multiple_of(t * TILE, TILE), TILE)
        rows = xa[0:width, at].astype(F32)
        squares = jnp.sum(rows * rows, axis=0, keepdims=True)
        xa[tail_start:PAD_D, at] = with_norms(
            xa[tail_start:PAD_D, at].astype(F32), squares, tail_used, tail_used + 3, 0).astype(BF16)

    y_rsz(1)
    y_agz(0)
    r_agx(0)
    r_agx_pass(0)
    y_agz(1)
    ag2_start("y", y_block, 0)
    r_rsx(1)
    for i in (0, 2):
        arrived("r_agx", 0, i)
    for i in range(1, NY * NK):
        arrived("b", 0, i)
    waits["b"].wait()
    pbuf[0, :, 0:PAD_R] = inverse_times(0, rbuf[0], 1)
    partial_start(0)
    ag2_start("y", y_block, 1)
    u_agz(0)
    r_rsz(1)
    ag3_start("y", y_block, 0)
    ag3_start("y", y_block, 1)
    pass_start("y", y_block, 0)
    ag2_start("u", u_block, 0)
    r_agz(1)
    core_start("y", y_block, 0)
    pass_start("y", y_block, 1)
    ag3_start("u", u_block, 0)
    r_agx(1)
    r_agx_pass(1)
    core_start("y", y_block, 1)
    pass_start("u", u_block, 0)
    core_start("u", u_block, 0)
    for i in (0, 2):
        arrived("r_agx", 1, i)
    pbuf[1, :, 0:PAD_R] = inverse_times(1, rbuf[1], 1)
    core_end("y", 0)
    core_end("y", 1)

    second = ybuf[1, c].reshape(PICK, PAD_D)
    tail = second[:, tail_start:PAD_D].astype(F32)
    lane = lax.broadcasted_iota(jnp.int32, tail.shape, 1)
    turned = pltpu.roll(tail, 125, 1)
    tail = jnp.where((lane >= tail_used) & (lane < tail_used + 3), turned, tail)
    tail = jnp.where((lane >= tail_used + 3) & (lane < tail_used + 6), 1.0, tail)
    second = jnp.concatenate([second[:, :tail_start], tail.astype(BF16)], axis=1)
    for j in range(4):
        inner = dot_t(second, ybuf[0, 2 * j:2 * j + 2].reshape(512, PAD_D))
        k21[:, j * 512:(j + 1) * 512] = jnp.exp2(inner * scale).astype(BF16)
    same = jnp.where(owners[0] == owners[1], 0.5, 0.0).astype(F32)
    twice = jnp.where(idxc[1] == idxr[0:1, :], same, 0.0).astype(BF16)
    core_end("u", 0)
    moved = jnp.dot(k21[...], ubuf[0].reshape(BLOCK, PAD_C), preferred_element_type=F32)
    moved += jnp.dot(twice, ubuf[0, c].reshape(PICK, PAD_C), preferred_element_type=F32)
    pbuf[1] = pbuf[1] - inverse_times(1, moved, 0)
    partial_start(1)
    turn(0)
    mine = pl.ds(pl.multiple_of(c * PICK, PICK), PICK)

    def product(s, t, low, high):
        at = pl.ds(pl.multiple_of(t * 512, 512), 512)
        change = jnp.dot(ut[s, low:high, :], kb[s, :, at], preferred_element_type=F32)
        own = jnp.where(owners[s] == r, 1.0, 0.0).astype(F32)
        put = (picks(s, t * 512, 512) * own).astype(BF16)
        added = jnp.dot(ut[s, low:high, mine], put, preferred_element_type=F32)
        top = min(high, outs)
        res[low:top, at] = res[low:top, at] - (change + 0.5 * added)[:top - low, :]
        co[low:top, at] = co[low:top, at] + added[:top - low, :]

    def turn_half(h):
        ut[1, h * 128:(h + 1) * 128, :] = jnp.transpose(
            ubuf[1, :, :, :, :, h * 128:(h + 1) * 128].reshape(BLOCK, 128))

    def out_copies(t):
        at = pl.ds(pl.multiple_of(t * 512, 512), 512)
        return (pltpu.make_async_copy(res.at[:, at], res_out.at[:, at], osem.at[0, t]),
                pltpu.make_async_copy(co.at[:, at], co_out.at[:, at], osem.at[1, t]))

    gen(0, 0, 4)
    u_agz(1)
    gen(0, 4, 8)
    sends_done()
    copies[3].wait()
    ag2_start("u", u_block, 1)

    @pl.loop(0, 4)
    def _(t):
        product(0, t, 0, PAD_R)

    ag3_start("u", u_block, 1)
    gen(1, 0, 4)
    pass_start("u", u_block, 1)
    gen(1, 4, 8)
    sends_done()
    core_start("u", u_block, 1)
    for h, (low, high) in enumerate(((0, 128), (128, PAD_R))):
        @pl.when(k == h)
        def _():
            turn_half(h)

            @pl.loop(0, 4)
            def _(t):
                product(1, t, low, high)

    core_end("u", 1)
    for h, (low, high) in enumerate(((0, 128), (128, PAD_R))):
        @pl.when(k == 1 - h)
        def _():
            turn_half(h)

            @pl.loop(0, 4)
            def _(t):
                product(1, t, low, high)

                @pl.when(t > 0)
                def _():
                    for copy in out_copies(t - 1):
                        copy.start()

    for copy in out_copies(3):
        copy.start()
    sends_done()
    for t in range(4):
        for copy in out_copies(t):
            copy.wait()


def per_device(features, residual, coeffs, block_inverse, block_index, owners):
    frames, width = features.shape
    outs = residual.shape[1]
    vmem = pl.BlockSpec(memory_space=pltpu.VMEM)
    new_coeffs, new_residual = pl.pallas_call(
        functools.partial(body, width, outs),
        out_shape=(jax.ShapeDtypeStruct((outs, frames), F32),
                   jax.ShapeDtypeStruct((outs, frames), F32)),
        in_specs=[pl.BlockSpec(memory_space=pltpu.SMEM)] + [pl.BlockSpec(memory_space=pl.ANY)] * 4 + [vmem],
        out_specs=(pl.BlockSpec(memory_space=pl.ANY),) * 2,
        scratch_shapes=[
            pltpu.VMEM((2, PICK, 1), jnp.int32),
            pltpu.VMEM((outs, BLOCK), F32),
            pltpu.VMEM((outs, BLOCK), F32),
            pltpu.VMEM((2, 8, BLOCK), F32),
            pltpu.VMEM((PAD_D, BLOCK), BF16),
            pltpu.VMEM((2, PICK, PAD_D), BF16),
            pltpu.VMEM((2, PAD_R, PICK), F32),
            pltpu.VMEM((NX, 40, PICK), F32),
            pltpu.VMEM((NX, 40, PICK), F32),
            pltpu.VMEM((2, 40, PICK), F32),
            pltpu.VMEM((NZ, 8, PICK), F32),
            pltpu.VMEM((NZ, 8, PICK), F32),
            pltpu.VMEM((2, 8, PICK), F32),
            pltpu.VMEM((2, PAD_R, PICK), F32),
            pltpu.VMEM((NX, NK, 64, 256), BF16),
            pltpu.VMEM((NX, NK, 64, 256), BF16),
            pltpu.VMEM((2, NK, 64, 256), BF16),
            pltpu.VMEM((NZ, 16, 256), BF16),
            pltpu.VMEM((NZ, 16, 256), BF16),
            pltpu.VMEM((2, 16, 256), BF16),
            pltpu.VMEM((2, 8, NX, 64, PAD_D), BF16),
            pltpu.VMEM((2, 64, PICK), F32),
            pltpu.VMEM((2, 64, PAD_C), F32),
            pltpu.VMEM((2, 8, 16, 128), F32),
            pltpu.VMEM((2, 16, 128), BF16),
            pltpu.VMEM((2, NZ, NX, NY, 16, PAD_C), BF16),
            pltpu.VMEM((2, PAD_C, BLOCK), BF16),
            pltpu.VMEM((2, BLOCK, BLOCK), BF16),
            pltpu.VMEM((PICK, BLOCK), BF16),
            pltpu.SemaphoreType.DMA((N_SEMS,)),
            pltpu.SemaphoreType.DMA((N_SEMS,)),
            pltpu.SemaphoreType.DMA((24,)),
            pltpu.SemaphoreType.DMA((2, 4)),
        ],
        compiler_params=pltpu.CompilerParams(
            collective_id=0, has_side_effects=True, vmem_limit_bytes=50 * 1024 * 1024),
        name="steps",
    )(*[pltpu.with_memory_space_constraint(v, pltpu.HBM) for v in
          (owners, features.T, residual.T, coeffs.T, block_inverse, block_index)])
    return new_coeffs.T, new_residual.T


def solution(mesh):
    both = ("rows", "cols")
    in_specs = (P(both, None), P(both, None), P(both, None), P(None, both, None),
                P(None, "cols"), P())
    out_specs = (P(both, None), P(both, None))
    return jax.shard_map(per_device, mesh=mesh, in_specs=in_specs, out_specs=out_specs,
                         check_vma=False)
```
